32 devices in a mesh: seqb: 4 (over x, core), seqt: 2 (over y), ch: 4 (over z).
Axes of the slice: x: 2, y: 2, z: 4, core: 2. Of those that a mesh axis runs over, the one named last changes fastest.
Arguments:
- query_gate: bfloat16 [2048, 4096], P(('seqb', 'seqt'), 'ch'), may hold values from -6 to 6
- key_proj: bfloat16 [2048, 4096], P(('seqb', 'seqt'), 'ch'), may hold values from -6 to 6
- value_proj: bfloat16 [2048, 4096], P(('seqb', 'seqt'), 'ch'), may hold values from -6 to 6
- filters: float32 [2048, 4096], P(('seqb', 'seqt'), 'ch'), may hold values from -4 to 4
- skip_gain: float32 [4096], P('ch'), may hold values from 0.5 to 2
- w_out: bfloat16 [4096, 4096], P('ch', ('seqb', 'seqt')), may hold values from -0.09375 to 0.09375
Outputs:
- layer_out: bfloat16 [2048, 4096], P(('seqb', 'seqt'), 'ch')
The draws below stay inside these ranges and needn't reach their ends.
All inputs are finite; a program needn't handle non-finite values.
Results may differ from the reference program's by a relative error of at most 0.0049.
Values may be sent and summed in bfloat16 or wider, within the bound.
A program may use at most 128 MiB of HBM per device.

```python
import math
import jax
import jax.numpy as jnp
from jax import lax

D = 4096
TOKENS = 2048


def draw_filters(key, part):
    base = jax.random.fold_in(key, 31)
    rate_key, value_key = jax.random.split(base)
    position = jnp.arange(TOKENS, dtype=jnp.float32)[:, None]
    log_rate = jax.random.uniform(rate_key, (1, D), jnp.float32, math.log(0.3 / TOKENS), math.log(1.0 / 30.0))
    values = jnp.clip(jax.random.normal(value_key, (TOKENS, D), jnp.float32), -4.0, 4.0)
    rate = jnp.exp(log_rate)
    return values * jnp.exp(-rate * position) * jnp.sqrt(1.0 - jnp.exp(-2.0 * rate))


def level_of(rng, dims, cuts, least, largest):
    def one(dim, shards_of):
        steps = jax.random.uniform(jax.random.fold_in(jax.random.fold_in(rng, 6), dim), (shards_of,), jnp.float32, least / len(cuts), largest / len(cuts))
        return jnp.repeat(jnp.exp(steps), dims[dim] // shards_of).reshape((-1,) + (1,) * (len(dims) - dim - 1))

    factor_of = one(*cuts[0])
    for cut in cuts[1:]:
        factor_of = factor_of * one(*cut)
    return factor_of


def scatter_about(own_key, extent, spread, bound, cuts=(), kind=jnp.bfloat16):
    entries = spread * jax.random.normal(own_key, extent, jnp.float32)
    if cuts:
        entries = entries * level_of(own_key, extent, cuts, -0.22, 0.18)
    return jnp.clip(entries, -bound, bound).astype(kind)


def setup_inputs(seed: int = 0) -> dict:
    seeds = jax.random.split(jax.random.key(seed), 7)
    query_gate = scatter_about(seeds[0], (TOKENS, D), 1.0, 6.0, ((0, 8), (1, 4)))
    key_proj = scatter_about(seeds[1], (TOKENS, D), 1.0, 6.0, ((0, 8), (1, 4)))
    value_proj = scatter_about(seeds[2], (TOKENS, D), 1.0, 6.0, ((0, 8), (1, 4)))
    filters = draw_filters(jax.random.fold_in(seeds[6], 71), 0)
    skip_gain = jnp.clip(0.5 + 1.5 * jax.random.uniform(seeds[4], (D,), jnp.float32) ** level_of(seeds[4], (D,), ((0, 4),), -0.2, 0.2), 0.5, 2.0)
    w_out = scatter_about(seeds[5], (D, D), D ** -0.5, 0.09375, ((0, 4), (1, 8)))
    return dict(query_gate=query_gate, key_proj=key_proj, value_proj=value_proj, filters=filters, skip_gain=skip_gain, w_out=w_out)


def reference(query_gate, key_proj, value_proj, filters, skip_gain, w_out):
    product = key_proj.astype(jnp.float32) * value_proj.astype(jnp.float32)
    block_width = min(D, 256)
    block_count = D // block_width

    def convolve_block(block_pair):
        signal_block, filter_block = block_pair
        spectrum = jnp.fft.rfft(signal_block, n=2 * TOKENS, axis=0)
        response = jnp.fft.rfft(filter_block, n=2 * TOKENS, axis=0)
        return jnp.fft.irfft(spectrum * response, n=2 * TOKENS, axis=0)[:TOKENS].astype(jnp.float32)

    signal_blocks = product.reshape(TOKENS, block_count, block_width).transpose(1, 0, 2)
    filter_blocks = filters.astype(jnp.float32).reshape(TOKENS, block_count, block_width).transpose(1, 0, 2)
    convolved = lax.map(convolve_block, (signal_blocks, filter_blocks))
    convolved = convolved.transpose(1, 0, 2).reshape(TOKENS, D)
    gated_rows = (query_gate.astype(jnp.float32) * (convolved + skip_gain[None, :] * product)).astype(jnp.bfloat16)
    return jnp.dot(gated_rows, w_out, preferred_element_type=jnp.float32).astype(jnp.bfloat16)
```

```python
import numpy as np

import jax
import jax.numpy as jnp
from jax import lax
from jax.experimental import pallas as pl
from jax.experimental.pallas import tpu as pltpu
from jax.sharding import PartitionSpec as P

SEQ = ("seqb", "seqt")


def split(x):
    hi = x.astype(jnp.bfloat16)
    return hi, (x - hi.astype(jnp.float32)).astype(jnp.bfloat16)


def dot32(m_hi, m_lo, a):
    a_hi, a_lo = split(a)
    dot = lambda p, q: jnp.dot(p, q, preferred_element_type=jnp.float32)
    return dot(m_hi, a_hi) + dot(m_lo, a_hi) + dot(m_hi, a_lo)


def conv_kernel(coef_ref, x_ref, base_ref, twid_ref, out_ref, acc_ref):
    blocks, rows, both = x_ref.shape
    width = both // 2
    k = pl.program_id(0)

    @pl.when(k == 0)
    def _():
        acc_ref[...] = jnp.zeros_like(acc_ref)

    re = jnp.zeros((rows, both), jnp.float32)
    im = jnp.zeros((rows, both), jnp.float32)
    for n in range(blocks):
        x = x_ref[n].astype(jnp.float32)
        re += coef_ref[0, k, n] * x
        im -= coef_ref[1, k, n] * x
    tc = twid_ref[0, :, 0:1]
    ts = twid_ref[0, :, 1:2]
    a = jnp.concatenate([re * tc + im * ts, im * tc - re * ts], axis=1)
    p = dot32(base_ref[0], base_ref[1], a)
    q = dot32(base_ref[2], base_ref[3], a)
    br = p[:, :both] + q[:, both:]
    bi = p[:, both:] - q[:, :both]
    sr, fr = br[:, :width], br[:, width:]
    si, fi = bi[:, :width], bi[:, width:]
    y = jnp.concatenate([sr * fr - si * fi, sr * fi + si * fr], axis=1)
    p = dot32(base_ref[0], base_ref[1], y)
    q = dot32(base_ref[2], base_ref[3], y)
    zr = p[:, :width] - q[:, width:]
    zi = p[:, width:] + q[:, :width]
    vr = zr * tc - zi * ts
    vi = zi * tc + zr * ts
    for n in range(blocks):
        acc_ref[n] += coef_ref[2, k, n] * vr - coef_ref[3, k, n] * vi

    @pl.when(k == blocks)
    def _():
        out_ref[...] = acc_ref[...].astype(out_ref.dtype)


def tables(blocks, rows):
    period = 2 * blocks * rows
    k = np.arange(blocks + 1)
    n = np.arange(blocks)
    ang = 2 * np.pi * ((k[:, None] * n[None, :]) % (2 * blocks)) / (2 * blocks)
    gain = np.where((k == 0) | (k == blocks), 1.0, 2.0)[:, None] / period
    coef = np.stack([np.cos(ang), np.sin(ang), gain * np.cos(ang), gain * np.sin(ang)])
    r = np.arange(rows)
    ang = 2 * np.pi * ((r[:, None] * r[None, :]) % rows) / rows
    parts = []
    for m in (np.cos(ang), np.sin(ang)):
        hi = m.astype(jnp.bfloat16)
        parts += [hi, (m - hi.astype(np.float64)).astype(jnp.bfloat16)]
    ang = 2 * np.pi * ((k[:, None] * r[None, :]) % period) / period
    twid = np.stack([np.cos(ang), np.sin(ang)], axis=-1)
    return coef.astype(np.float32), np.stack(parts), twid.astype(np.float32)


def convolve(columns):
    blocks, rows, both = columns.shape
    coef, base, twid = tables(blocks, rows)
    return pl.pallas_call(
        conv_kernel,
        grid=(blocks + 1,),
        out_shape=jax.ShapeDtypeStruct((blocks, rows, both // 2), jnp.bfloat16),
        in_specs=[
            pl.BlockSpec(memory_space=pltpu.SMEM),
            pl.BlockSpec((blocks, rows, both), lambda k: (0, 0, 0)),
            pl.BlockSpec((4, rows, rows), lambda k: (0, 0, 0)),
            pl.BlockSpec((1, rows, 2), lambda k: (k, 0, 0)),
        ],
        out_specs=pl.BlockSpec((blocks, rows, both // 2), lambda k: (0, 0, 0)),
        scratch_shapes=[pltpu.VMEM((blocks, rows, both // 2), jnp.float32)],
        compiler_params=pltpu.CompilerParams(vmem_limit_bytes=48 * 1024 * 1024),
        cost_estimate=pl.CostEstimate(
            flops=36 * (blocks + 1) * rows * rows * both, bytes_accessed=4 * 1024 * 1024, transcendentals=0
        ),
    )(jnp.asarray(coef), columns, jnp.asarray(base), jnp.asarray(twid))


MESH = pl.DeviceIdType.MESH
LANES = 128
HALF = float(np.sqrt(0.5))
COS = [float(np.cos(np.pi * n / 8)) for n in range(4)]
SIN = [float(np.sin(np.pi * n / 8)) for n in range(4)]


def forward16(x):
    a = [x[n] + x[n + 4] for n in range(4)]
    b = [x[n] - x[n + 4] for n in range(4)]
    s, t = a[0] + a[2], a[1] + a[3]
    u, w = HALF * (b[1] - b[3]), HALF * (b[1] + b[3])
    even = {
        0: (s + t, None),
        8: (s - t, None),
        4: (a[0] - a[2], a[3] - a[1]),
        2: (b[0] + u, -b[2] - w),
        6: (b[0] - u, b[2] - w),
    }
    ur, ui = [x[0]], [-x[4]]
    for n in range(1, 4):
        ur.append(COS[n] * x[n] - SIN[n] * x[n + 4])
        ui.append(-COS[n] * x[n + 4] - SIN[n] * x[n])
    t0r, t0i, t1r, t1i = ur[0] + ur[2], ui[0] + ui[2], ur[0] - ur[2], ui[0] - ui[2]
    t2r, t2i, t3r, t3i = ur[1] + ur[3], ui[1] + ui[3], ur[1] - ur[3], ui[1] - ui[3]
    odd = {
        1: (t0r + t2r, t0i + t2i),
        7: (t0r - t2r, t2i - t0i),
        5: (t1r + t3i, t1i - t3r),
        3: (t1r - t3i, -t1i - t3r),
    }
    return {**even, **odd}


def backward16(re, im):
    s, t = re[0] + re[8], re[0] - re[8]
    p = [s + re[4], t - im[4], s - re[4], t + im[4]]
    u, w = HALF * (re[2] - re[6]), HALF * (im[2] + im[6])
    q = [re[2] + re[6], u - w, im[6] - im[2], -u - w]
    w1r, w1i, w5r, w5i = re[1], im[1], re[5], im[5]
    w9r, w9i, w13r, w13i = re[7], -im[7], re[3], -im[3]
    ar, ai, br, bi = w1r + w9r, w1i + w9i, w1r - w9r, w1i - w9i
    cr, ci, dr, di = w5r + w13r, w5i + w13i, w5r - w13r, w5i - w13i
    gr = [ar + cr, br - di, ar - cr, br + di]
    gi = [ai + ci, bi + dr, ai - ci, bi - dr]
    low, high = [], []
    for n in range(4):
        if n == 0:
            o, r = gr[0], -gi[0]
        else:
            o = COS[n] * gr[n] - SIN[n] * gi[n]
            r = -COS[n] * gi[n] - SIN[n] * gr[n]
        low.append(p[n] + q[n] + o)
        high.append(p[n] - q[n] + r)
    return low + high


def layer_kernel(q_hbm, k_hbm, v_hbm, f_hbm, skip_ref, w_hbm, base_hbm, twid_hbm, out_ref,
                 q_ref, k_ref, v_ref, f_ref, base_ref, twid_ref,
                 xs_send, xs_recv, a_ref, y_ref, f_spec, v_spec, cs_send, cs_recv, g_ref, w_all,
                 p_send, p_recv, p_own, p_far, r_recv, o_send, o_recv,
                 load_s, own_s, in_s, in_r, back_s, back_r, g_s, g_r, w_s, w_r,
                 p_s, p_r, r_r, o_s, o_r):
    blocks = lax.axis_size("seqb") * lax.axis_size("seqt")
    depth = lax.axis_size("ch")
    ib, it, z = lax.axis_index("seqb"), lax.axis_index("seqt"), lax.axis_index("ch")
    me = ib * 2 + it
    core, chip = ib % 2, ib // 2
    rows, channels = k_ref.shape
    width = channels // blocks
    cols = w_hbm.shape[1]
    chunks = cols // LANES
    half = rows // 2
    f32, bf16 = jnp.float32, jnp.bfloat16
    flips = [ib, ib + 1 - 2 * core, (ib + 2) % 4, 3 - ib]
    peers = [(a, t) for a, t in ((2, 1), (3, 1), (2, 0), (0, 1), (3, 0), (1, 1), (1, 0))]
    place = [{"seqb": flips[a], "seqt": it if t == 0 else 1 - it} for a, t in peers]
    index = [flips[a] * 2 + (it if t == 0 else 1 - it) for a, t in peers]
    sibling = {"seqb": flips[1]}
    over_x = {"seqb": flips[2]}
    over_y = {"seqb": flips[1], "seqt": 1 - it}

    def remote(src, dst, send, recv, where):
        return pltpu.make_async_remote_copy(
            src_ref=src, dst_ref=dst, send_sem=send, recv_sem=recv, device_id=where, device_id_type=MESH
        )

    loads = [
        pltpu.make_async_copy(src, dst, load_s.at[i])
        for i, (src, dst) in enumerate(
            ((f_hbm, f_ref), (k_hbm, k_ref), (v_hbm, v_ref), (base_hbm, base_ref), (twid_hbm, twid_ref), (q_hbm, q_ref))
        )
    ]
    own = [
        pltpu.make_async_copy(w_hbm.at[:, pl.ds(j * LANES, LANES)], w_all.at[0, j], own_s.at[j])
        for j in range(chunks)
    ]
    for copy in loads:
        copy.start()

    barrier = pltpu.get_barrier_semaphore()
    for where in place:
        pl.semaphore_signal(barrier, inc=1, device_id=where, device_id_type=MESH)
    for j in range(1, depth):
        pl.semaphore_signal(barrier, inc=1, device_id={"ch": (z + j) % depth}, device_id_type=MESH)

    def lanes_of(d):
        return pl.ds(pl.multiple_of(d * width, width), width)

    def filter_piece(d):
        return f_ref[:, lanes_of(d)].astype(bf16)

    def product_piece(d):
        return (k_ref[:, lanes_of(d)].astype(f32) * v_ref[:, lanes_of(d)].astype(f32)).astype(bf16)

    entry = []
    for s, piece in enumerate((filter_piece, product_piece)):
        for copy in loads[:1] if s == 0 else loads[1:3]:
            copy.wait()
        for i in range(len(peers)):
            xs_send[s, i] = piece(index[i])
        if s == 0:
            pl.semaphore_wait(barrier, blocks + depth - 2)
        for i in range(len(peers)):
            copy = remote(xs_send.at[s, i], xs_recv.at[s, me], in_s.at[s, i], in_r.at[s, i], place[i])
            copy.start()
            entry.append(copy)
        xs_recv[s, me] = piece(me)
    for copy in own:
        copy.start()

    def weight_x(j):
        return remote(w_hbm.at[:, pl.ds(j * LANES, LANES)], w_all.at[1, j], w_s.at[0, j], w_r.at[1, j], over_x)

    def weight_y(j):
        return remote(w_hbm.at[:, pl.ds(j * LANES, LANES)], w_all.at[2, j], w_s.at[1, j], w_r.at[2, j], over_y)

    def weight_on(j):
        if j < chunks // 2:
            return remote(w_all.at[2, j], w_all.at[3, j], w_s.at[2, j], w_r.at[3, j], over_x)
        return remote(w_all.at[1, j], w_all.at[3, j], w_s.at[2, j], w_r.at[3, j], over_y)

    x_order = list(range(chunks // 2, chunks)) + list(range(chunks // 2))
    y_order = list(range(chunks))
    EARLY = 1
    for j in range(EARLY):
        weight_x(x_order[j]).start()
        weight_y(y_order[j]).start()

    for copy in loads[3:5]:
        copy.wait()

    tile = 16

    def put(dst, k, start, lane, value):
        hi, lo = split(value)
        span = slice(lane * LANES, (lane + 1) * LANES)
        dst[k, pl.ds(start, tile), span] = hi
        dst[k, pl.ds(rows + start, tile), span] = hi
        dst[k, pl.ds(2 * rows + start, tile), span] = lo

    def spread(s):
        def body(i, carry):
            start = pl.multiple_of(i * tile, tile)
            span = pl.ds(start, tile)
            out = forward16([xs_recv[s, n, span, :].astype(f32) for n in range(blocks)])
            for k in range(blocks + 1):
                re, im = out[k]
                if k == 0:
                    im = jnp.zeros_like(re)
                else:
                    tc, ts = twid_ref[0, k, span, :], twid_ref[1, k, span, :]
                    if im is None:
                        re, im = re * tc, -re * ts
                    else:
                        re, im = re * tc + im * ts, im * tc - re * ts
                put(a_ref, k, start, 0, re)
                put(a_ref, k, start, 1, im)
            return carry

        lax.fori_loop(0, rows // tile, body, 0)

    def transform(value):
        d = jnp.dot(base_ref[...], value, preferred_element_type=f32)
        return d[:rows, :LANES], d[:rows, LANES:], d[rows:, :LANES], d[rows:, LANES:]

    for copy in entry[: len(peers)]:
        copy.wait_recv()
    spread(0)
    scale = 1.0 / (2 * blocks * rows)

    def filter_step(k, carry):
        cr, ci, sr, si = transform(a_ref[k])
        gain = jnp.where((k == 0) | (k == blocks), scale, 2 * scale)
        f_spec[0, k] = (cr + si) * gain
        f_spec[1, k] = (ci - sr) * gain
        return carry

    lax.fori_loop(0, blocks + 1, filter_step, 0, unroll=3)

    for copy in entry[len(peers):]:
        copy.wait_recv()
    spread(1)

    def signal_step(k, carry):
        cr, ci, sr, si = transform(a_ref[k])
        xr, xi = cr + si, ci - sr
        fr, fi = f_spec[0, k], f_spec[1, k]
        y = jnp.concatenate([xr * fr - xi * fi, xr * fi + xi * fr], axis=1)
        hi, lo = split(y)
        y_ref[k, 0:rows] = hi
        y_ref[k, rows:2 * rows] = hi
        y_ref[k, 2 * rows:3 * rows] = lo
        cr, ci, sr, si = transform(y_ref[k])
        zr, zi = cr - si, ci + sr
        tc, ts = twid_ref[0, k], twid_ref[1, k]
        v_spec[0, k] = zr * tc - zi * ts
        v_spec[1, k] = zi * tc + zr * ts
        return carry

    lax.fori_loop(0, blocks + 1, signal_step, 0, unroll=3)

    def gather_points(h):
        def body(i, carry):
            span = pl.ds(pl.multiple_of(h * half + i * tile, tile), tile)
            re = [v_spec[0, k, span, :] for k in range(blocks + 1)]
            im = [v_spec[1, k, span, :] for k in range(blocks + 1)]
            for n, value in enumerate(backward16(re, im)):
                cs_send[n, span, :] = value.astype(bf16)
            return carry

        lax.fori_loop(0, half // tile, body, 0)

    back = [[], []]
    for h in range(2):
        gather_points(h)
        span = pl.ds(h * half, half)
        for i in range(len(peers)):
            copy = remote(
                cs_send.at[index[i], span], cs_recv.at[me, span], back_s.at[h, i], back_r.at[h, i], place[i]
            )
            copy.start()
            back[h].append(copy)
        cs_recv[me, span] = cs_send[me, span]
    for j in range(EARLY, chunks):
        weight_x(x_order[j]).start()
        weight_y(y_order[j]).start()

    loads[5].wait()
    swaps = []
    for h in range(2):
        for copy in back[h]:
            copy.wait_recv()
        span = slice(h * half, (h + 1) * half)
        there = pl.ds(pl.multiple_of(core * rows + h * half, half), half)
        for d in range(blocks):
            lanes = slice(d * width, (d + 1) * width)
            p = k_ref[span, lanes].astype(f32) * v_ref[span, lanes].astype(f32)
            conv = cs_recv[d, span, :].astype(f32)
            g_ref[there, lanes] = (
                q_ref[span, lanes].astype(f32) * (conv + skip_ref[:, lanes] * p)
            ).astype(bf16)
        swap = remote(g_ref.at[there], g_ref.at[there], g_s.at[h], g_r.at[h], sibling)
        swap.start()
        swaps.append(swap)
    for swap in swaps:
        swap.wait()

    goal = [chip * 2 + core, (1 - chip) * 2 + core, chip * 2 + 1 - core, (1 - chip) * 2 + 1 - core]
    beside = z + 1 - 2 * (z % 2)
    outer = (z == 0) | (z == 3)
    inner = jnp.logical_not(outer)
    across = jnp.where(z < 2, 2, 1)

    def direct(c, j):
        slot = jnp.where(c == beside, 0, 1)
        return remote(p_send.at[c, j], p_recv.at[slot, j], p_s.at[c, j], p_r.at[slot, j], {"ch": c})

    def relay(c, j):
        return remote(p_send.at[c, j], r_recv.at[c % 2, j], p_s.at[c, j], r_r.at[c % 2, j], {"ch": beside})

    units = [(0, j) for j in range(chunks)]
    for i in range(chunks):
        units += [(1, x_order[i]), (2, y_order[i])]
    for i in range(chunks // 2):
        units += [(3, i), (3, chunks // 2 + i)]

    def finish(unit):
        kind, j = unit
        c = goal[kind]

        @pl.when(inner & (c != z) & (c != beside))
        def _():
            relay(c, j).wait_recv()
            p_send[c, j] = (p_far[c % 2, j] + r_recv[c % 2, j].astype(f32)).astype(bf16)
            direct(c, j).start()

    LAG = 2
    for n, (kind, j) in enumerate(units):
        c = goal[kind]
        if kind == 0:
            own[j].wait()
        else:
            remote(w_all.at[0, j], w_all.at[kind, j], w_s.at[0, j], w_r.at[kind, j], over_x).wait_recv()
        if (kind == 2 and j < chunks // 2) or (kind == 1 and j >= chunks // 2):
            weight_on(j).start()
        part = jnp.dot(g_ref[...], w_all[kind, j], preferred_element_type=f32)

        @pl.when(c == z)
        def _():
            p_own[j] = part

        @pl.when(inner & (c != z) & (c != beside))
        def _():
            p_far[c % 2, j] = part

        @pl.when(c == beside)
        def _():
            p_send[c, j] = part.astype(bf16)
            direct(c, j).start()

        @pl.when(outer & (c != z) & (c != beside))
        def _():
            p_send[c, j] = part.astype(bf16)
            relay(c, j).start()

        if n >= LAG:
            finish(units[n - LAG])
    for unit in units[-LAG:]:
        finish(unit)

    side = jnp.where(z % 2 == core, it, 1 - it)
    last = []
    mine = pl.ds(pl.multiple_of(core * rows, rows), rows)
    theirs = pl.ds(pl.multiple_of((1 - core) * rows, rows), rows)

    def total(j, span):
        s = p_own[j, span, :] + p_recv[0, j, span, :].astype(f32)
        return (s + p_recv[1, j, span, :].astype(f32)).astype(bf16)

    for j in range(chunks):
        for slot in range(2):
            remote(p_send.at[0, j], p_recv.at[slot, j], p_s.at[0, j], p_r.at[slot, j], sibling).wait_recv()
        o_send[j] = total(j, theirs)
        copy = remote(o_send.at[j], o_recv.at[j], o_s.at[j], o_r.at[j], sibling)
        copy.start()
        last.append(copy)
        out_ref[:, pl.ds(pl.multiple_of(side * cols + j * LANES, LANES), LANES)] = total(j, mine)
    for j in range(chunks):
        last[j].wait()
        out_ref[:, pl.ds(pl.multiple_of((1 - side) * cols + j * LANES, LANES), LANES)] = o_recv[j]

    for copy in entry + back[0] + back[1]:
        copy.wait_send()
    for j in range(chunks):
        weight_x(j).wait_send()
        weight_y(j).wait_send()
        weight_on(j).wait_send()
        for kind in range(4):
            c = goal[kind]

            @pl.when(c != z)
            def _():
                remote(p_send.at[c, j], p_send.at[c, j], p_s.at[c, j], p_r.at[0, j], sibling).wait_send()


def fused(query_gate, key_proj, value_proj, filters, skip_gain, w_out):
    rows, channels = key_proj.shape
    cols = w_out.shape[1]
    blocks = lax.axis_size(SEQ)
    depth = lax.axis_size("ch")
    width = channels // blocks
    _, base, twid = tables(blocks, rows)
    cos_hi, cos_lo, sin_hi, sin_lo = base
    base = np.concatenate(
        [np.concatenate([cos_hi, cos_lo, cos_hi], axis=1), np.concatenate([sin_hi, sin_lo, sin_hi], axis=1)], axis=0
    )
    twid = np.broadcast_to(twid.transpose(2, 0, 1)[..., None], (2, blocks + 1, rows, LANES))
    chunks = cols // LANES
    bf16, f32 = jnp.bfloat16, jnp.float32
    dma = pltpu.SemaphoreType.DMA
    anywhere, vmem = pl.BlockSpec(memory_space=pl.ANY), pl.BlockSpec(memory_space=pltpu.VMEM)
    return pl.pallas_call(
        layer_kernel,
        out_shape=jax.ShapeDtypeStruct((rows, channels), bf16),
        in_specs=[anywhere] * 4 + [vmem] + [anywhere] * 3,
        out_specs=vmem,
        scratch_shapes=[
            pltpu.VMEM((rows, channels), bf16),
            pltpu.VMEM((rows, channels), bf16),
            pltpu.VMEM((rows, channels), bf16),
            pltpu.VMEM((rows, channels), f32),
            pltpu.VMEM(base.shape, bf16),
            pltpu.VMEM(twid.shape, f32),
            pltpu.VMEM((2, blocks - 1, rows, width), bf16),
            pltpu.VMEM((2, blocks, rows, width), bf16),
            pltpu.VMEM((blocks + 1, 3 * rows, 2 * width), bf16),
            pltpu.VMEM((blocks + 1, 3 * rows, 2 * width), bf16),
            pltpu.VMEM((2, blocks + 1, rows, width), f32),
            pltpu.VMEM((2, blocks + 1, rows, width), f32),
            pltpu.VMEM((blocks, rows, width), bf16),
            pltpu.VMEM((blocks, rows, width), bf16),
            pltpu.VMEM((2 * rows, channels), bf16),
            pltpu.VMEM((4, chunks, channels, LANES), bf16),
            pltpu.VMEM((depth, chunks, 2 * rows, LANES), bf16),
            pltpu.VMEM((2, chunks, 2 * rows, LANES), bf16),
            pltpu.VMEM((chunks, 2 * rows, LANES), f32),
            pltpu.VMEM((2, chunks, 2 * rows, LANES), f32),
            pltpu.VMEM((2, chunks, 2 * rows, LANES), bf16),
            pltpu.VMEM((chunks, rows, LANES), bf16),
            pltpu.VMEM((chunks, rows, LANES), bf16),
            dma((6,)), dma((chunks,)),
            dma((2, blocks - 1)), dma((2, blocks - 1)),
            dma((2, blocks - 1)), dma((2, blocks - 1)),
            dma((2,)), dma((2,)),
            dma((3, chunks)), dma((4, chunks)),
            dma((depth, chunks)), dma((2, chunks)), dma((2, chunks)),
            dma((chunks,)), dma((chunks,)),
        ],
        compiler_params=pltpu.CompilerParams(
            collective_id=0, has_side_effects=True, vmem_limit_bytes=56 * 1024 * 1024
        ),
    )(query_gate, key_proj, value_proj, filters, skip_gain[None, :], w_out, jnp.asarray(base), jnp.asarray(twid))


def shards(query_gate, key_proj, value_proj, filters, skip_gain, w_out):
    rows, channels = key_proj.shape
    seq = lax.axis_size(SEQ)
    width = channels // seq
    if (width, w_out.shape[1] % 256, seq, lax.axis_size("seqb"), lax.axis_size("ch")) == (128, 0, 8, 4, 4):
        return fused(query_gate, key_proj, value_proj, filters, skip_gain, w_out)
    product = key_proj.astype(jnp.float32) * value_proj.astype(jnp.float32)
    pieces = lambda a: a.astype(jnp.bfloat16).reshape(rows, seq, width).transpose(1, 0, 2)
    stacked = jnp.concatenate([pieces(product), pieces(filters)], axis=2)
    columns = lax.all_to_all(stacked, SEQ, split_axis=0, concat_axis=0, tiled=True)
    spatial = lax.all_to_all(convolve(columns), SEQ, split_axis=0, concat_axis=0, tiled=True)
    convolved = spatial.transpose(1, 0, 2).reshape(rows, channels).astype(jnp.float32)
    gated_rows = (
        query_gate.astype(jnp.float32) * (convolved + skip_gain[None, :] * product)
    ).astype(jnp.bfloat16)
    weights = lax.all_gather(w_out, SEQ, axis=1, tiled=True)
    partial_sums = jnp.dot(gated_rows, weights, preferred_element_type=jnp.float32)
    return lax.psum_scatter(partial_sums, "ch", scatter_dimension=1, tiled=True).astype(
        jnp.bfloat16
    )


def solution(mesh):
    return jax.shard_map(
        shards,
        mesh=mesh,
        in_specs=(
            P(SEQ, "ch"),
            P(SEQ, "ch"),
            P(SEQ, "ch"),
            P(SEQ, "ch"),
            P("ch"),
            P("ch", SEQ),
        ),
        out_specs=P(SEQ, "ch"),
        check_vma=False,
    )
```

```python
import numpy as np

import jax
import jax.numpy as jnp
from jax import lax
from jax.experimental import pallas as pl
from jax.experimental.pallas import tpu as pltpu
from jax.sharding import PartitionSpec as P

SEQ = ("seqb", "seqt")


def split(x):
    hi = x.astype(jnp.bfloat16)
    return hi, (x - hi.astype(jnp.float32)).astype(jnp.bfloat16)


def dot32(m_hi, m_lo, a):
    a_hi, a_lo = split(a)
    dot = lambda p, q: jnp.dot(p, q, preferred_element_type=jnp.float32)
    return dot(m_hi, a_hi) + dot(m_lo, a_hi) + dot(m_hi, a_lo)


def conv_kernel(coef_ref, x_ref, base_ref, twid_ref, out_ref, acc_ref):
    blocks, rows, both = x_ref.shape
    width = both // 2
    k = pl.program_id(0)

    @pl.when(k == 0)
    def _():
        acc_ref[...] = jnp.zeros_like(acc_ref)

    re = jnp.zeros((rows, both), jnp.float32)
    im = jnp.zeros((rows, both), jnp.float32)
    for n in range(blocks):
        x = x_ref[n].astype(jnp.float32)
        re += coef_ref[0, k, n] * x
        im -= coef_ref[1, k, n] * x
    tc = twid_ref[0, :, 0:1]
    ts = twid_ref[0, :, 1:2]
    a = jnp.concatenate([re * tc + im * ts, im * tc - re * ts], axis=1)
    p = dot32(base_ref[0], base_ref[1], a)
    q = dot32(base_ref[2], base_ref[3], a)
    br = p[:, :both] + q[:, both:]
    bi = p[:, both:] - q[:, :both]
    sr, fr = br[:, :width], br[:, width:]
    si, fi = bi[:, :width], bi[:, width:]
    y = jnp.concatenate([sr * fr - si * fi, sr * fi + si * fr], axis=1)
    p = dot32(base_ref[0], base_ref[1], y)
    q = dot32(base_ref[2], base_ref[3], y)
    zr = p[:, :width] - q[:, width:]
    zi = p[:, width:] + q[:, :width]
    vr = zr * tc - zi * ts
    vi = zi * tc + zr * ts
    for n in range(blocks):
        acc_ref[n] += coef_ref[2, k, n] * vr - coef_ref[3, k, n] * vi

    @pl.when(k == blocks)
    def _():
        out_ref[...] = acc_ref[...].astype(out_ref.dtype)


def tables(blocks, rows):
    period = 2 * blocks * rows
    k = np.arange(blocks + 1)
    n = np.arange(blocks)
    ang = 2 * np.pi * ((k[:, None] * n[None, :]) % (2 * blocks)) / (2 * blocks)
    gain = np.where((k == 0) | (k == blocks), 1.0, 2.0)[:, None] / period
    coef = np.stack([np.cos(ang), np.sin(ang), gain * np.cos(ang), gain * np.sin(ang)])
    r = np.arange(rows)
    ang = 2 * np.pi * ((r[:, None] * r[None, :]) % rows) / rows
    parts = []
    for m in (np.cos(ang), np.sin(ang)):
        hi = m.astype(jnp.bfloat16)
        parts += [hi, (m - hi.astype(np.float64)).astype(jnp.bfloat16)]
    ang = 2 * np.pi * ((k[:, None] * r[None, :]) % period) / period
    twid = np.stack([np.cos(ang), np.sin(ang)], axis=-1)
    return coef.astype(np.float32), np.stack(parts), twid.astype(np.float32)


def convolve(columns):
    blocks, rows, both = columns.shape
    coef, base, twid = tables(blocks, rows)
    return pl.pallas_call(
        conv_kernel,
        grid=(blocks + 1,),
        out_shape=jax.ShapeDtypeStruct((blocks, rows, both // 2), jnp.bfloat16),
        in_specs=[
            pl.BlockSpec(memory_space=pltpu.SMEM),
            pl.BlockSpec((blocks, rows, both), lambda k: (0, 0, 0)),
            pl.BlockSpec((4, rows, rows), lambda k: (0, 0, 0)),
            pl.BlockSpec((1, rows, 2), lambda k: (k, 0, 0)),
        ],
        out_specs=pl.BlockSpec((blocks, rows, both // 2), lambda k: (0, 0, 0)),
        scratch_shapes=[pltpu.VMEM((blocks, rows, both // 2), jnp.float32)],
        compiler_params=pltpu.CompilerParams(vmem_limit_bytes=48 * 1024 * 1024),
        cost_estimate=pl.CostEstimate(
            flops=36 * (blocks + 1) * rows * rows * both, bytes_accessed=4 * 1024 * 1024, transcendentals=0
        ),
    )(jnp.asarray(coef), columns, jnp.asarray(base), jnp.asarray(twid))


MESH = pl.DeviceIdType.MESH
LANES = 128
HALF = float(np.sqrt(0.5))
COS = [float(np.cos(np.pi * n / 8)) for n in range(4)]
SIN = [float(np.sin(np.pi * n / 8)) for n in range(4)]


def forward16(x):
    a = [x[n] + x[n + 4] for n in range(4)]
    b = [x[n] - x[n + 4] for n in range(4)]
    s, t = a[0] + a[2], a[1] + a[3]
    u, w = HALF * (b[1] - b[3]), HALF * (b[1] + b[3])
    even = {
        0: (s + t, None),
        8: (s - t, None),
        4: (a[0] - a[2], a[3] - a[1]),
        2: (b[0] + u, -b[2] - w),
        6: (b[0] - u, b[2] - w),
    }
    ur, ui = [x[0]], [-x[4]]
    for n in range(1, 4):
        ur.append(COS[n] * x[n] - SIN[n] * x[n + 4])
        ui.append(-COS[n] * x[n + 4] - SIN[n] * x[n])
    t0r, t0i, t1r, t1i = ur[0] + ur[2], ui[0] + ui[2], ur[0] - ur[2], ui[0] - ui[2]
    t2r, t2i, t3r, t3i = ur[1] + ur[3], ui[1] + ui[3], ur[1] - ur[3], ui[1] - ui[3]
    odd = {
        1: (t0r + t2r, t0i + t2i),
        7: (t0r - t2r, t2i - t0i),
        5: (t1r + t3i, t1i - t3r),
        3: (t1r - t3i, -t1i - t3r),
    }
    return {**even, **odd}


def backward16(re, im):
    s, t = re[0] + re[8], re[0] - re[8]
    p = [s + re[4], t - im[4], s - re[4], t + im[4]]
    u, w = HALF * (re[2] - re[6]), HALF * (im[2] + im[6])
    q = [re[2] + re[6], u - w, im[6] - im[2], -u - w]
    w1r, w1i, w5r, w5i = re[1], im[1], re[5], im[5]
    w9r, w9i, w13r, w13i = re[7], -im[7], re[3], -im[3]
    ar, ai, br, bi = w1r + w9r, w1i + w9i, w1r - w9r, w1i - w9i
    cr, ci, dr, di = w5r + w13r, w5i + w13i, w5r - w13r, w5i - w13i
    gr = [ar + cr, br - di, ar - cr, br + di]
    gi = [ai + ci, bi + dr, ai - ci, bi - dr]
    low, high = [], []
    for n in range(4):
        if n == 0:
            o, r = gr[0], -gi[0]
        else:
            o = COS[n] * gr[n] - SIN[n] * gi[n]
            r = -COS[n] * gi[n] - SIN[n] * gr[n]
        low.append(p[n] + q[n] + o)
        high.append(p[n] - q[n] + r)
    return low + high


def layer_kernel(q_hbm, k_hbm, v_hbm, f_hbm, skip_ref, w_hbm, base_hbm, twid_hbm, out_ref,
                 q_ref, k_ref, v_ref, f_ref, base_ref, angle_ref, twid_ref,
                 xs_send, xs_recv, a_ref, y_ref, f_spec, v_spec, cs_send, cs_recv, g_ref, w_all,
                 p_send, p_recv, p_own, p_far, r_recv, o_send, o_recv,
                 load_s, own_s, in_s, in_r, back_s, back_r, g_s, g_r, w_s, w_r,
                 p_s, p_r, r_r, o_s, o_r):
    blocks = lax.axis_size("seqb") * lax.axis_size("seqt")
    depth = lax.axis_size("ch")
    ib, it, z = lax.axis_index("seqb"), lax.axis_index("seqt"), lax.axis_index("ch")
    me = ib * 2 + it
    core, chip = ib % 2, ib // 2
    rows, channels = k_ref.shape
    width = channels // blocks
    cols = w_hbm.shape[1]
    chunks = cols // LANES
    half = rows // 2
    f32, bf16 = jnp.float32, jnp.bfloat16
    flips = [ib, ib + 1 - 2 * core, (ib + 2) % 4, 3 - ib]
    peers = [(a, t) for a, t in ((2, 1), (3, 1), (2, 0), (0, 1), (3, 0), (1, 1), (1, 0))]
    place = [{"seqb": flips[a], "seqt": it if t == 0 else 1 - it} for a, t in peers]
    index = [flips[a] * 2 + (it if t == 0 else 1 - it) for a, t in peers]
    sibling = {"seqb": flips[1]}
    over_x = {"seqb": flips[2]}
    over_y = {"seqb": flips[1], "seqt": 1 - it}

    def remote(src, dst, send, recv, where):
        return pltpu.make_async_remote_copy(
            src_ref=src, dst_ref=dst, send_sem=send, recv_sem=recv, device_id=where, device_id_type=MESH
        )

    loads = [
        pltpu.make_async_copy(src, dst, load_s.at[i])
        for i, (src, dst) in enumerate(
            ((f_hbm, f_ref), (k_hbm, k_ref), (v_hbm, v_ref), (twid_hbm, angle_ref), (base_hbm, base_ref), (q_hbm, q_ref))
        )
    ]
    x_order = list(range(chunks // 2, chunks)) + list(range(chunks // 2))
    y_order = list(range(chunks))
    units = [((0, 2 * i), (0, 2 * i + 1)) for i in range(chunks // 2)]
    straight = [((1, x_order[i]), (2, y_order[i])) for i in range(chunks)]
    diagonal = [((3, i), (3, chunks // 2 + i)) for i in range(chunks // 2)]
    early, late = straight[:chunks // 2], straight[chunks // 2:]
    units += early + [pair for both in zip(diagonal, late) for pair in both]

    def store(kind, j):
        for p, pair in enumerate(units):
            if (kind, j) in pair:
                return w_all.at[p, :, pl.ds(pair.index((kind, j)) * LANES, LANES)]

    own = [
        pltpu.make_async_copy(w_hbm.at[:, pl.ds(2 * i * LANES, 2 * LANES)], w_all.at[i], own_s.at[i])
        for i in range(chunks // 2)
    ]
    for copy in loads:
        copy.start()

    barrier = pltpu.get_barrier_semaphore()
    for where in place:
        pl.semaphore_signal(barrier, inc=1, device_id=where, device_id_type=MESH)
    for j in range(1, depth):
        pl.semaphore_signal(barrier, inc=1, device_id={"ch": (z + j) % depth}, device_id_type=MESH)

    def lanes_of(d):
        return pl.ds(pl.multiple_of(d * width, width), width)

    def filter_piece(d):
        return f_ref[:, lanes_of(d)].astype(bf16)

    def product_piece(d):
        return (k_ref[:, lanes_of(d)].astype(f32) * v_ref[:, lanes_of(d)].astype(f32)).astype(bf16)

    entry = []
    for s, piece in enumerate((filter_piece, product_piece)):
        for copy in loads[:1] if s == 0 else loads[1:3]:
            copy.wait()
        for i in range(len(peers)):
            xs_send[s, i] = piece(index[i])
        if s == 0:
            pl.semaphore_wait(barrier, blocks + depth - 2)
        for i in range(len(peers)):
            copy = remote(xs_send.at[s, i], xs_recv.at[s, me], in_s.at[s, i], in_r.at[s, i], place[i])
            copy.start()
            entry.append(copy)
        xs_recv[s, me] = piece(me)
    for copy in own:
        copy.start()

    def weight_x(j):
        return remote(w_hbm.at[:, pl.ds(j * LANES, LANES)], store(1, j), w_s.at[0, j], w_r.at[1, j], over_x)

    def weight_y(j):
        return remote(w_hbm.at[:, pl.ds(j * LANES, LANES)], store(2, j), w_s.at[1, j], w_r.at[2, j], over_y)

    def weight_on(j):
        if j < chunks // 2:
            return remote(store(2, j), store(3, j), w_s.at[2, j], w_r.at[3, j], over_x)
        return remote(store(1, j), store(3, j), w_s.at[2, j], w_r.at[3, j], over_y)

    def weight_ready(kind, j):
        remote(store(kind, j), store(kind, j), w_s.at[0, j], w_r.at[kind, j], over_x).wait_recv()

    EARLY = 1
    for j in range(EARLY):
        weight_x(x_order[j]).start()
        weight_y(y_order[j]).start()

    loads[3].wait()
    for c in range(2):
        for k in range(blocks + 1):
            column = c * (blocks + 1) + k
            twid_ref[c, k] = jnp.broadcast_to(angle_ref[:, column:column + 1], (rows, LANES))
    loads[4].wait()

    tile = 16

    def put(dst, k, start, lane, value):
        hi, lo = split(value)
        span = slice(lane * LANES, (lane + 1) * LANES)
        dst[k, pl.ds(start, tile), span] = hi
        dst[k, pl.ds(rows + start, tile), span] = hi
        dst[k, pl.ds(2 * rows + start, tile), span] = lo

    def spread(s):
        def body(i, carry):
            start = pl.multiple_of(i * tile, tile)
            span = pl.ds(start, tile)
            out = forward16([xs_recv[s, n, span, :].astype(f32) for n in range(blocks)])
            for k in range(blocks + 1):
                re, im = out[k]
                if k == 0:
                    im = jnp.zeros_like(re)
                else:
                    tc, ts = twid_ref[0, k, span, :], twid_ref[1, k, span, :]
                    if im is None:
                        re, im = re * tc, -re * ts
                    else:
                        re, im = re * tc + im * ts, im * tc - re * ts
                put(a_ref, k, start, 0, re)
                put(a_ref, k, start, 1, im)
            return carry

        lax.fori_loop(0, rows // tile, body, 0)

    def transform(value, h):
        d = jnp.dot(base_ref[h * rows:(h + 1) * rows], value, preferred_element_type=f32)
        return d[:half, :LANES], d[:half, LANES:], d[half:, :LANES], d[half:, LANES:]

    for copy in entry[: len(peers)]:
        copy.wait_recv()
    spread(0)
    scale = 1.0 / (2 * blocks * rows)

    def filter_step(k):
        for h in range(2):
            span = slice(h * half, (h + 1) * half)
            cr, ci, sr, si = transform(a_ref[k], h)
            gain = scale if k in (0, blocks) else 2 * scale
            f_spec[0, k, span] = (cr + si) * gain
            f_spec[1, k, span] = (ci - sr) * gain

    for k in range(blocks + 1):
        filter_step(k)

    for copy in entry[len(peers):]:
        copy.wait_recv()
    spread(1)

    def signal_step(k):
        for h in range(2):
            span = slice(h * half, (h + 1) * half)
            cr, ci, sr, si = transform(a_ref[k], h)
            xr, xi = cr + si, ci - sr
            fr, fi = f_spec[0, k, span], f_spec[1, k, span]
            for e, y in enumerate((xr * fr - xi * fi, xr * fi + xi * fr)):
                lanes = slice(e * LANES, (e + 1) * LANES)
                hi, lo = split(y)
                y_ref[k, h * half:(h + 1) * half, lanes] = hi
                y_ref[k, rows + h * half:rows + (h + 1) * half, lanes] = hi
                y_ref[k, 2 * rows + h * half:2 * rows + (h + 1) * half, lanes] = lo

    def inverse_step(k, h):
        span = slice(h * half, (h + 1) * half)
        cr, ci, sr, si = transform(y_ref[k], h)
        zr, zi = cr - si, ci + sr
        tc, ts = twid_ref[0, k, span], twid_ref[1, k, span]
        v_spec[0, k, span] = zr * tc - zi * ts
        v_spec[1, k, span] = zi * tc + zr * ts

    for k in range(blocks + 1):
        signal_step(k)

    def gather_points(h):
        def body(i, carry):
            span = pl.ds(pl.multiple_of(h * half + i * tile, tile), tile)
            re = [v_spec[0, k, span, :] for k in range(blocks + 1)]
            im = [v_spec[1, k, span, :] for k in range(blocks + 1)]
            for n, value in enumerate(backward16(re, im)):
                cs_send[n, span, :] = value.astype(bf16)
            return carry

        lax.fori_loop(0, half // tile, body, 0)

    back = [[], []]
    for h in range(2):
        for k in range(blocks + 1):
            inverse_step(k, h)
        gather_points(h)
        span = pl.ds(h * half, half)
        for i in range(len(peers)):
            copy = remote(
                cs_send.at[index[i], span], cs_recv.at[me, span], back_s.at[h, i], back_r.at[h, i], place[i]
            )
            copy.start()
            back[h].append(copy)
        cs_recv[me, span] = cs_send[me, span]
    pending = []
    for i in range(chunks // 2):
        pending += [(weight_on(y_order[i]), weight_on(x_order[i]))]
        pending += [(weight_x(x_order[chunks // 2 + i]), weight_y(y_order[chunks // 2 + i]))]
    for i in range(EARLY, chunks // 2):
        weight_x(x_order[i]).start()
        weight_y(y_order[i]).start()

    def pass_on(i):
        for kind, j in early[i]:
            weight_ready(kind, j)
        for pair in pending[2 * i:2 * i + 2]:
            for copy in pair:
                copy.start()

    for i in range(EARLY):
        pass_on(i)

    goal = [chip * 2 + core, (1 - chip) * 2 + core, chip * 2 + 1 - core, (1 - chip) * 2 + 1 - core]
    beside = z + 1 - 2 * (z % 2)
    outer = (z == 0) | (z == 3)
    inner = jnp.logical_not(outer)
    whole = slice(0, 2 * rows)

    def direct(c, j, span=whole):
        slot = jnp.where(c == beside, 0, 1)
        return remote(
            p_send.at[c, j, span], p_recv.at[slot, j, span], p_s.at[c, j], p_r.at[slot, j], {"ch": c}
        )

    def relay(c, j, span=whole):
        return remote(
            p_send.at[c, j, span], r_recv.at[c % 2, j, span], p_s.at[c, j], r_r.at[c % 2, j], {"ch": beside}
        )

    def finish(unit):
        kind, j = unit
        c = goal[kind]

        @pl.when(inner & (c != z) & (c != beside))
        def _():
            relay(c, j).wait_recv()
            p_send[c, j] = (p_far[c % 2, j] + r_recv[c % 2, j].astype(f32)).astype(bf16)
            direct(c, j).start()

    def product(p, span):
        both = jnp.dot(g_ref[span], w_all[p], preferred_element_type=f32)
        for e, (kind, j) in enumerate(units[p]):
            part = both[:, e * LANES:(e + 1) * LANES]
            c = goal[kind]

            @pl.when(c == z)
            def _():
                p_own[j, span] = part

            @pl.when(inner & (c != z) & (c != beside))
            def _():
                p_far[c % 2, j, span] = part

            @pl.when((outer & (c != z)) | (c == beside))
            def _():
                p_send[c, j, span] = part.astype(bf16)

            @pl.when(c == beside)
            def _():
                direct(c, j, span).start()

            @pl.when(outer & (c != z) & (c != beside))
            def _():
                relay(c, j, span).start()

    loads[5].wait()
    swaps = []
    for h in range(2):
        for copy in back[h]:
            copy.wait_recv()
        span = slice(h * half, (h + 1) * half)
        there = pl.ds(pl.multiple_of(h * rows + core * half, half), half)
        for d in range(blocks):
            lanes = slice(d * width, (d + 1) * width)
            p = k_ref[span, lanes].astype(f32) * v_ref[span, lanes].astype(f32)
            conv = cs_recv[d, span, :].astype(f32)
            g_ref[there, lanes] = (
                q_ref[span, lanes].astype(f32) * (conv + skip_ref[:, lanes] * p)
            ).astype(bf16)
        swap = remote(g_ref.at[there], g_ref.at[there], g_s.at[h], g_r.at[h], sibling)
        swap.start()
        swaps.append(swap)
        swap.wait_recv()
        for p in range(chunks // 2):
            if h == 0:
                own[p].wait()
            product(p, slice(h * rows, (h + 1) * rows))

    queue = [unit for p in range(chunks // 2) for unit in units[p]]
    for p in range(chunks // 2, 2 * chunks):
        if units[p] not in early:
            for kind, j in units[p]:
                weight_ready(kind, j)
        elif early.index(units[p]) >= EARLY:
            pass_on(early.index(units[p]))
        product(p, whole)
        for unit in queue[:2]:
            finish(unit)
        queue = queue[2:] + list(units[p])

    for unit in queue:
        finish(unit)

    side = jnp.where(z % 2 == core, it, 1 - it)
    last = []

    def total(j, whose):
        parts = []
        for h in range(2):
            span = pl.ds(pl.multiple_of(h * rows + whose * half, half), half)
            s = p_own[j, span, :] + p_recv[0, j, span, :].astype(f32)
            parts.append((s + p_recv[1, j, span, :].astype(f32)).astype(bf16))
        return jnp.concatenate(parts, axis=0)

    for j in range(chunks):
        for slot in range(2):
            remote(p_send.at[0, j], p_recv.at[slot, j], p_s.at[0, j], p_r.at[slot, j], sibling).wait_recv()
        o_send[j] = total(j, 1 - core)
        copy = remote(o_send.at[j], o_recv.at[j], o_s.at[j], o_r.at[j], sibling)
        copy.start()
        last.append(copy)
        out_ref[:, pl.ds(pl.multiple_of(side * cols + j * LANES, LANES), LANES)] = total(j, core)
    for j in range(chunks):
        last[j].wait()
        out_ref[:, pl.ds(pl.multiple_of((1 - side) * cols + j * LANES, LANES), LANES)] = o_recv[j]

    for copy in entry + back[0] + back[1] + swaps:
        copy.wait_send()
    for j in range(chunks):
        weight_x(j).wait_send()
        weight_y(j).wait_send()
        weight_on(j).wait_send()
        for kind in range(4):
            c = goal[kind]

            @pl.when(c != z)
            def _():
                remote(p_send.at[c, j], p_send.at[c, j], p_s.at[c, j], p_r.at[0, j], sibling).wait_send()


def fused(query_gate, key_proj, value_proj, filters, skip_gain, w_out):
    rows, channels = key_proj.shape
    cols = w_out.shape[1]
    blocks = lax.axis_size(SEQ)
    depth = lax.axis_size("ch")
    width = channels // blocks
    _, base, twid = tables(blocks, rows)
    cos_hi, cos_lo, sin_hi, sin_lo = base
    base = np.stack(
        [np.concatenate([cos_hi, cos_lo, cos_hi], axis=1), np.concatenate([sin_hi, sin_lo, sin_hi], axis=1)]
    )
    base = base.reshape(2, 2, rows // 2, 3 * rows).swapaxes(0, 1).reshape(2 * rows, 3 * rows)
    twid = np.pad(twid.transpose(1, 2, 0).reshape(rows, -1), ((0, 0), (0, LANES - 2 * (blocks + 1))))
    chunks = cols // LANES
    bf16, f32 = jnp.bfloat16, jnp.float32
    dma = pltpu.SemaphoreType.DMA
    anywhere, vmem = pl.BlockSpec(memory_space=pl.ANY), pl.BlockSpec(memory_space=pltpu.VMEM)
    return pl.pallas_call(
        layer_kernel,
        out_shape=jax.ShapeDtypeStruct((rows, channels), bf16),
        in_specs=[anywhere] * 4 + [vmem] + [anywhere] * 3,
        out_specs=vmem,
        scratch_shapes=[
            pltpu.VMEM((rows, channels), bf16),
            pltpu.VMEM((rows, channels), bf16),
            pltpu.VMEM((rows, channels), bf16),
            pltpu.VMEM((rows, channels), f32),
            pltpu.VMEM(base.shape, bf16),
            pltpu.VMEM(twid.shape, f32),
            pltpu.VMEM((2, blocks + 1, rows, LANES), f32),
            pltpu.VMEM((2, blocks - 1, rows, width), bf16),
            pltpu.VMEM((2, blocks, rows, width), bf16),
            pltpu.VMEM((blocks + 1, 3 * rows, 2 * width), bf16),
            pltpu.VMEM((blocks + 1, 3 * rows, 2 * width), bf16),
            pltpu.VMEM((2, blocks + 1, rows, width), f32),
            pltpu.VMEM((2, blocks + 1, rows, width), f32),
            pltpu.VMEM((blocks, rows, width), bf16),
            pltpu.VMEM((blocks, rows, width), bf16),
            pltpu.VMEM((2 * rows, channels), bf16),
            pltpu.VMEM((2 * chunks, channels, 2 * LANES), bf16),
            pltpu.VMEM((depth, chunks, 2 * rows, LANES), bf16),
            pltpu.VMEM((2, chunks, 2 * rows, LANES), bf16),
            pltpu.VMEM((chunks, 2 * rows, LANES), f32),
            pltpu.VMEM((2, chunks, 2 * rows, LANES), f32),
            pltpu.VMEM((2, chunks, 2 * rows, LANES), bf16),
            pltpu.VMEM((chunks, rows, LANES), bf16),
            pltpu.VMEM((chunks, rows, LANES), bf16),
            dma((6,)), dma((chunks,)),
            dma((2, blocks - 1)), dma((2, blocks - 1)),
            dma((2, blocks - 1)), dma((2, blocks - 1)),
            dma((2,)), dma((2,)),
            dma((3, chunks)), dma((4, chunks)),
            dma((depth, chunks)), dma((2, chunks)), dma((2, chunks)),
            dma((chunks,)), dma((chunks,)),
        ],
        compiler_params=pltpu.CompilerParams(
            collective_id=0, has_side_effects=True, vmem_limit_bytes=56 * 1024 * 1024
        ),
    )(query_gate, key_proj, value_proj, filters, skip_gain[None, :], w_out, jnp.asarray(base), jnp.asarray(twid))


def shards(query_gate, key_proj, value_proj, filters, skip_gain, w_out):
    rows, channels = key_proj.shape
    seq = lax.axis_size(SEQ)
    width = channels // seq
    if (width, w_out.shape[1] % 256, seq, lax.axis_size("seqb"), lax.axis_size("ch")) == (128, 0, 8, 4, 4):
        return fused(query_gate, key_proj, value_proj, filters, skip_gain, w_out)
    product = key_proj.astype(jnp.float32) * value_proj.astype(jnp.float32)
    pieces = lambda a: a.astype(jnp.bfloat16).reshape(rows, seq, width).transpose(1, 0, 2)
    stacked = jnp.concatenate([pieces(product), pieces(filters)], axis=2)
    columns = lax.all_to_all(stacked, SEQ, split_axis=0, concat_axis=0, tiled=True)
    spatial = lax.all_to_all(convolve(columns), SEQ, split_axis=0, concat_axis=0, tiled=True)
    convolved = spatial.transpose(1, 0, 2).reshape(rows, channels).astype(jnp.float32)
    gated_rows = (
        query_gate.astype(jnp.float32) * (convolved + skip_gain[None, :] * product)
    ).astype(jnp.bfloat16)
    weights = lax.all_gather(w_out, SEQ, axis=1, tiled=True)
    partial_sums = jnp.dot(gated_rows, weights, preferred_element_type=jnp.float32)
    return lax.psum_scatter(partial_sums, "ch", scatter_dimension=1, tiled=True).astype(
        jnp.bfloat16
    )


def solution(mesh):
    return jax.shard_map(
        shards,
        mesh=mesh,
        in_specs=(
            P(SEQ, "ch"),
            P(SEQ, "ch"),
            P(SEQ, "ch"),
            P(SEQ, "ch"),
            P("ch"),
            P("ch", SEQ),
        ),
        out_specs=P(SEQ, "ch"),
        check_vma=False,
    )
```

```python
import numpy as np

import jax
import jax.numpy as jnp
from jax import lax
from jax.experimental import pallas as pl
from jax.experimental.pallas import tpu as pltpu
from jax.sharding import PartitionSpec as P

SEQ = ("seqb", "seqt")


def split(x):
    hi = x.astype(jnp.bfloat16)
    return hi, (x - hi.astype(jnp.float32)).astype(jnp.bfloat16)


def dot32(m_hi, m_lo, a):
    a_hi, a_lo = split(a)
    dot = lambda p, q: jnp.dot(p, q, preferred_element_type=jnp.float32)
    return dot(m_hi, a_hi) + dot(m_lo, a_hi) + dot(m_hi, a_lo)


def conv_kernel(coef_ref, x_ref, base_ref, twid_ref, out_ref, acc_ref):
    blocks, rows, both = x_ref.shape
    width = both // 2
    k = pl.program_id(0)

    @pl.when(k == 0)
    def _():
        acc_ref[...] = jnp.zeros_like(acc_ref)

    re = jnp.zeros((rows, both), jnp.float32)
    im = jnp.zeros((rows, both), jnp.float32)
    for n in range(blocks):
        x = x_ref[n].astype(jnp.float32)
        re += coef_ref[0, k, n] * x
        im -= coef_ref[1, k, n] * x
    tc = twid_ref[0, :, 0:1]
    ts = twid_ref[0, :, 1:2]
    a = jnp.concatenate([re * tc + im * ts, im * tc - re * ts], axis=1)
    p = dot32(base_ref[0], base_ref[1], a)
    q = dot32(base_ref[2], base_ref[3], a)
    br = p[:, :both] + q[:, both:]
    bi = p[:, both:] - q[:, :both]
    sr, fr = br[:, :width], br[:, width:]
    si, fi = bi[:, :width], bi[:, width:]
    y = jnp.concatenate([sr * fr - si * fi, sr * fi + si * fr], axis=1)
    p = dot32(base_ref[0], base_ref[1], y)
    q = dot32(base_ref[2], base_ref[3], y)
    zr = p[:, :width] - q[:, width:]
    zi = p[:, width:] + q[:, :width]
    vr = zr * tc - zi * ts
    vi = zi * tc + zr * ts
    for n in range(blocks):
        acc_ref[n] += coef_ref[2, k, n] * vr - coef_ref[3, k, n] * vi

    @pl.when(k == blocks)
    def _():
        out_ref[...] = acc_ref[...].astype(out_ref.dtype)


def tables(blocks, rows):
    period = 2 * blocks * rows
    k = np.arange(blocks + 1)
    n = np.arange(blocks)
    ang = 2 * np.pi * ((k[:, None] * n[None, :]) % (2 * blocks)) / (2 * blocks)
    gain = np.where((k == 0) | (k == blocks), 1.0, 2.0)[:, None] / period
    coef = np.stack([np.cos(ang), np.sin(ang), gain * np.cos(ang), gain * np.sin(ang)])
    r = np.arange(rows)
    ang = 2 * np.pi * ((r[:, None] * r[None, :]) % rows) / rows
    parts = []
    for m in (np.cos(ang), np.sin(ang)):
        hi = m.astype(jnp.bfloat16)
        parts += [hi, (m - hi.astype(np.float64)).astype(jnp.bfloat16)]
    ang = 2 * np.pi * ((k[:, None] * r[None, :]) % period) / period
    twid = np.stack([np.cos(ang), np.sin(ang)], axis=-1)
    return coef.astype(np.float32), np.stack(parts), twid.astype(np.float32)


def convolve(columns):
    blocks, rows, both = columns.shape
    coef, base, twid = tables(blocks, rows)
    return pl.pallas_call(
        conv_kernel,
        grid=(blocks + 1,),
        out_shape=jax.ShapeDtypeStruct((blocks, rows, both // 2), jnp.bfloat16),
        in_specs=[
            pl.BlockSpec(memory_space=pltpu.SMEM),
            pl.BlockSpec((blocks, rows, both), lambda k: (0, 0, 0)),
            pl.BlockSpec((4, rows, rows), lambda k: (0, 0, 0)),
            pl.BlockSpec((1, rows, 2), lambda k: (k, 0, 0)),
        ],
        out_specs=pl.BlockSpec((blocks, rows, both // 2), lambda k: (0, 0, 0)),
        scratch_shapes=[pltpu.VMEM((blocks, rows, both // 2), jnp.float32)],
        compiler_params=pltpu.CompilerParams(vmem_limit_bytes=48 * 1024 * 1024),
        cost_estimate=pl.CostEstimate(
            flops=36 * (blocks + 1) * rows * rows * both, bytes_accessed=4 * 1024 * 1024, transcendentals=0
        ),
    )(jnp.asarray(coef), columns, jnp.asarray(base), jnp.asarray(twid))


MESH = pl.DeviceIdType.MESH
LANES = 128
HALF = float(np.sqrt(0.5))
COS = [float(np.cos(np.pi * n / 8)) for n in range(4)]
SIN = [float(np.sin(np.pi * n / 8)) for n in range(4)]


def forward16(x):
    a = [x[n] + x[n + 4] for n in range(4)]
    b = [x[n] - x[n + 4] for n in range(4)]
    s, t = a[0] + a[2], a[1] + a[3]
    u, w = HALF * (b[1] - b[3]), HALF * (b[1] + b[3])
    even = {
        0: (s + t, None),
        8: (s - t, None),
        4: (a[0] - a[2], a[3] - a[1]),
        2: (b[0] + u, -b[2] - w),
        6: (b[0] - u, b[2] - w),
    }
    ur, ui = [x[0]], [-x[4]]
    for n in range(1, 4):
        ur.append(COS[n] * x[n] - SIN[n] * x[n + 4])
        ui.append(-COS[n] * x[n + 4] - SIN[n] * x[n])
    t0r, t0i, t1r, t1i = ur[0] + ur[2], ui[0] + ui[2], ur[0] - ur[2], ui[0] - ui[2]
    t2r, t2i, t3r, t3i = ur[1] + ur[3], ui[1] + ui[3], ur[1] - ur[3], ui[1] - ui[3]
    odd = {
        1: (t0r + t2r, t0i + t2i),
        7: (t0r - t2r, t2i - t0i),
        5: (t1r + t3i, t1i - t3r),
        3: (t1r - t3i, -t1i - t3r),
    }
    return {**even, **odd}


def backward16(re, im):
    s, t = re[0] + re[8], re[0] - re[8]
    p = [s + re[4], t - im[4], s - re[4], t + im[4]]
    u, w = HALF * (re[2] - re[6]), HALF * (im[2] + im[6])
    q = [re[2] + re[6], u - w, im[6] - im[2], -u - w]
    w1r, w1i, w5r, w5i = re[1], im[1], re[5], im[5]
    w9r, w9i, w13r, w13i = re[7], -im[7], re[3], -im[3]
    ar, ai, br, bi = w1r + w9r, w1i + w9i, w1r - w9r, w1i - w9i
    cr, ci, dr, di = w5r + w13r, w5i + w13i, w5r - w13r, w5i - w13i
    gr = [ar + cr, br - di, ar - cr, br + di]
    gi = [ai + ci, bi + dr, ai - ci, bi - dr]
    low, high = [], []
    for n in range(4):
        if n == 0:
            o, r = gr[0], -gi[0]
        else:
            o = COS[n] * gr[n] - SIN[n] * gi[n]
            r = -COS[n] * gi[n] - SIN[n] * gr[n]
        low.append(p[n] + q[n] + o)
        high.append(p[n] - q[n] + r)
    return low + high


def layer_kernel(q_hbm, k_hbm, v_hbm, f_hbm, skip_ref, w_hbm, base_hbm, twid_hbm, out_ref,
                 q_ref, k_ref, v_ref, f_ref, base_ref, angle_ref, twid_ref,
                 xs_send, xs_recv, a_ref, y_ref, f_spec, v_spec, cs_send, cs_recv, g_ref, w_all,
                 p_send, p_recv, p_own, p_far, r_recv, o_send, o_recv,
                 load_s, own_s, in_s, in_r, back_s, back_r, g_s, g_r, w_s, w_r,
                 p_s, p_r, r_r, o_s, o_r):
    blocks = lax.axis_size("seqb") * lax.axis_size("seqt")
    depth = lax.axis_size("ch")
    ib, it, z = lax.axis_index("seqb"), lax.axis_index("seqt"), lax.axis_index("ch")
    me = ib * 2 + it
    core, chip = ib % 2, ib // 2
    rows, channels = k_ref.shape
    width = channels // blocks
    cols = w_hbm.shape[1]
    chunks = cols // LANES
    half = rows // 2
    f32, bf16 = jnp.float32, jnp.bfloat16
    flips = [ib, ib + 1 - 2 * core, (ib + 2) % 4, 3 - ib]
    peers = [(a, t) for a, t in ((2, 1), (3, 1), (2, 0), (0, 1), (3, 0), (1, 1), (1, 0))]
    place = [{"seqb": flips[a], "seqt": it if t == 0 else 1 - it} for a, t in peers]
    index = [flips[a] * 2 + (it if t == 0 else 1 - it) for a, t in peers]
    sibling = {"seqb": flips[1]}
    over_x = {"seqb": flips[2]}
    over_y = {"seqb": flips[1], "seqt": 1 - it}

    def remote(src, dst, send, recv, where):
        return pltpu.make_async_remote_copy(
            src_ref=src, dst_ref=dst, send_sem=send, recv_sem=recv, device_id=where, device_id_type=MESH
        )

    loads = [
        pltpu.make_async_copy(src, dst, load_s.at[i])
        for i, (src, dst) in enumerate(
            ((f_hbm, f_ref), (k_hbm, k_ref), (v_hbm, v_ref), (twid_hbm, angle_ref), (base_hbm, base_ref), (q_hbm, q_ref))
        )
    ]
    x_order = list(range(chunks // 2, chunks)) + list(range(chunks // 2))
    y_order = list(range(chunks))
    units = [((0, 2 * i), (0, 2 * i + 1)) for i in range(chunks // 2)]
    straight = [((1, x_order[i]), (2, y_order[i])) for i in range(chunks)]
    diagonal = [((3, i), (3, chunks // 2 + i)) for i in range(chunks // 2)]
    early, late = straight[:chunks // 2], straight[chunks // 2:]
    units += early + [pair for both in zip(diagonal, late) for pair in both]

    def store(kind, j):
        for p, pair in enumerate(units):
            if (kind, j) in pair:
                return w_all.at[p, :, pl.ds(pair.index((kind, j)) * LANES, LANES)]

    own = [
        pltpu.make_async_copy(w_hbm.at[:, pl.ds(2 * i * LANES, 2 * LANES)], w_all.at[i], own_s.at[i])
        for i in range(chunks // 2)
    ]
    for copy in loads:
        copy.start()

    barrier = pltpu.get_barrier_semaphore()
    for where in place:
        pl.semaphore_signal(barrier, inc=1, device_id=where, device_id_type=MESH)
    for j in range(1, depth):
        pl.semaphore_signal(barrier, inc=1, device_id={"ch": (z + j) % depth}, device_id_type=MESH)

    def lanes_of(d):
        return pl.ds(pl.multiple_of(d * width, width), width)

    def filter_piece(d):
        return f_ref[:, lanes_of(d)].astype(bf16)

    def product_piece(d):
        return (k_ref[:, lanes_of(d)].astype(f32) * v_ref[:, lanes_of(d)].astype(f32)).astype(bf16)

    entry = []
    for s, piece in enumerate((filter_piece, product_piece)):
        for copy in loads[:1] if s == 0 else loads[1:3]:
            copy.wait()
        for i in range(len(peers)):
            xs_send[s, i] = piece(index[i])
        if s == 0:
            pl.semaphore_wait(barrier, blocks + depth - 2)
        for i in range(len(peers)):
            copy = remote(xs_send.at[s, i], xs_recv.at[s, me], in_s.at[s, i], in_r.at[s, i], place[i])
            copy.start()
            entry.append(copy)
        xs_recv[s, me] = piece(me)
    for copy in own:
        copy.start()

    def weight_x(j):
        return remote(w_hbm.at[:, pl.ds(j * LANES, LANES)], store(1, j), w_s.at[0, j], w_r.at[1, j], over_x)

    def weight_y(j):
        return remote(w_hbm.at[:, pl.ds(j * LANES, LANES)], store(2, j), w_s.at[1, j], w_r.at[2, j], over_y)

    def weight_on(j):
        if j < chunks // 2:
            return remote(store(2, j), store(3, j), w_s.at[2, j], w_r.at[3, j], over_x)
        return remote(store(1, j), store(3, j), w_s.at[2, j], w_r.at[3, j], over_y)

    def weight_ready(kind, j):
        remote(store(kind, j), store(kind, j), w_s.at[0, j], w_r.at[kind, j], over_x).wait_recv()

    EARLY = 1
    for j in range(EARLY):
        weight_x(x_order[j]).start()
        weight_y(y_order[j]).start()

    loads[3].wait()
    for c in range(2):
        for k in range(blocks + 1):
            column = c * (blocks + 1) + k
            twid_ref[c, k] = jnp.broadcast_to(angle_ref[:, column:column + 1], (rows, LANES))
    loads[4].wait()

    tile = 16

    def put(dst, k, start, lane, value):
        hi, lo = split(value)
        span = slice(lane * LANES, (lane + 1) * LANES)
        dst[k, pl.ds(start, tile), span] = hi
        dst[k, pl.ds(rows + start, tile), span] = hi
        dst[k, pl.ds(2 * rows + start, tile), span] = lo

    def spread(s):
        def body(i, carry):
            start = pl.multiple_of(i * tile, tile)
            span = pl.ds(start, tile)
            out = forward16([xs_recv[s, n, span, :].astype(f32) for n in range(blocks)])
            for k in range(blocks + 1):
                re, im = out[k]
                if k == 0:
                    im = jnp.zeros_like(re)
                else:
                    tc, ts = twid_ref[0, k, span, :], twid_ref[1, k, span, :]
                    if im is None:
                        re, im = re * tc, -re * ts
                    else:
                        re, im = re * tc + im * ts, im * tc - re * ts
                put(a_ref, k, start, 0, re)
                put(a_ref, k, start, 1, im)
            return carry

        lax.fori_loop(0, rows // tile, body, 0)

    def transform(value, h):
        d = jnp.dot(base_ref[h * rows:(h + 1) * rows], value, preferred_element_type=f32)
        return d[:half, :LANES], d[:half, LANES:], d[half:, :LANES], d[half:, LANES:]

    for copy in entry[: len(peers)]:
        copy.wait_recv()
    spread(0)
    scale = 1.0 / (2 * blocks * rows)

    def filter_step(k):
        for h in range(2):
            span = slice(h * half, (h + 1) * half)
            cr, ci, sr, si = transform(a_ref[k], h)
            gain = scale if k in (0, blocks) else 2 * scale
            f_spec[0, k, span] = (cr + si) * gain
            f_spec[1, k, span] = (ci - sr) * gain

    for k in range(blocks + 1):
        filter_step(k)

    for copy in entry[len(peers):]:
        copy.wait_recv()
    spread(1)

    def signal_step(k):
        for h in range(2):
            span = slice(h * half, (h + 1) * half)
            cr, ci, sr, si = transform(a_ref[k], h)
            xr, xi = cr + si, ci - sr
            fr, fi = f_spec[0, k, span], f_spec[1, k, span]
            for e, y in enumerate((xr * fr - xi * fi, xr * fi + xi * fr)):
                lanes = slice(e * LANES, (e + 1) * LANES)
                hi, lo = split(y)
                y_ref[k, h * half:(h + 1) * half, lanes] = hi
                y_ref[k, rows + h * half:rows + (h + 1) * half, lanes] = hi
                y_ref[k, 2 * rows + h * half:2 * rows + (h + 1) * half, lanes] = lo

    def inverse_step(k, h):
        span = slice(h * half, (h + 1) * half)
        cr, ci, sr, si = transform(y_ref[k], h)
        zr, zi = cr - si, ci + sr
        tc, ts = twid_ref[0, k, span], twid_ref[1, k, span]
        v_spec[0, k, span] = zr * tc - zi * ts
        v_spec[1, k, span] = zi * tc + zr * ts

    for k in range(blocks + 1):
        signal_step(k)

    def gather_points(h):
        def body(i, carry):
            span = pl.ds(pl.multiple_of(h * half + i * tile, tile), tile)
            re = [v_spec[0, k, span, :] for k in range(blocks + 1)]
            im = [v_spec[1, k, span, :] for k in range(blocks + 1)]
            for n, value in enumerate(backward16(re, im)):
                cs_send[n, span, :] = value.astype(bf16)
            return carry

        lax.fori_loop(0, half // tile, body, 0)

    back = [[], []]
    for h in range(2):
        for k in range(blocks + 1):
            inverse_step(k, h)
        gather_points(h)
        span = pl.ds(h * half, half)
        for i in range(len(peers)):
            copy = remote(
                cs_send.at[index[i], span], cs_recv.at[me, span], back_s.at[h, i], back_r.at[h, i], place[i]
            )
            copy.start()
            back[h].append(copy)
        cs_recv[me, span] = cs_send[me, span]
    pending = []
    for i in range(chunks // 2):
        pending += [(weight_on(y_order[i]), weight_on(x_order[i]))]
        pending += [(weight_x(x_order[chunks // 2 + i]), weight_y(y_order[chunks // 2 + i]))]
    for i in range(EARLY, chunks // 2):
        weight_x(x_order[i]).start()
        weight_y(y_order[i]).start()

    def pass_on(i):
        for kind, j in early[i]:
            weight_ready(kind, j)
        for pair in pending[2 * i:2 * i + 2]:
            for copy in pair:
                copy.start()

    for i in range(EARLY):
        pass_on(i)

    goal = [chip * 2 + core, (1 - chip) * 2 + core, chip * 2 + 1 - core, (1 - chip) * 2 + 1 - core]
    beside = z + 1 - 2 * (z % 2)
    outer = (z == 0) | (z == 3)
    inner = jnp.logical_not(outer)
    whole = slice(0, 2 * rows)

    def direct(c, j, span=whole):
        slot = jnp.where(c == beside, 0, 1)
        return remote(
            p_send.at[c, j, span], p_recv.at[slot, j, span], p_s.at[c, j], p_r.at[slot, j], {"ch": c}
        )

    def relay(c, j, span=whole):
        return remote(
            p_send.at[c, j, span], r_recv.at[c % 2, j, span], p_s.at[c, j], r_r.at[c % 2, j], {"ch": beside}
        )

    def finish(unit):
        kind, j = unit
        c = goal[kind]

        @pl.when(inner & (c != z) & (c != beside))
        def _():
            relay(c, j).wait_recv()
            p_send[c, j] = (p_far[c % 2, j] + r_recv[c % 2, j].astype(f32)).astype(bf16)
            direct(c, j).start()

    def product(p, span):
        both = jnp.dot(g_ref[span], w_all[p], preferred_element_type=f32)
        for e, (kind, j) in enumerate(units[p]):
            part = both[:, e * LANES:(e + 1) * LANES]
            c = goal[kind]

            @pl.when(c == z)
            def _():
                p_own[j, span] = part

            @pl.when(inner & (c != z) & (c != beside))
            def _():
                p_far[c % 2, j, span] = part

            @pl.when((outer & (c != z)) | (c == beside))
            def _():
                p_send[c, j, span] = part.astype(bf16)

            @pl.when((c == beside) & inner if p in held else c == beside)
            def _():
                direct(c, j, span).start()

            @pl.when(outer & (c != z) & (c != beside))
            def _():
                relay(c, j, span).start()

    held = {1: 3, 2: 4, 3: 5, 4: 6, 5: 7, 6: 8, 7: 8}

    def release(step):
        for p in held:
            if held[p] == step:
                for kind, j in units[p]:
                    @pl.when(outer & (goal[kind] == beside))
                    def _():
                        direct(goal[kind], j).start()

    loads[5].wait()
    swaps = []
    for h in range(2):
        for copy in back[h]:
            copy.wait_recv()
        span = slice(h * half, (h + 1) * half)
        there = pl.ds(pl.multiple_of(h * rows + core * half, half), half)
        for d in range(blocks):
            lanes = slice(d * width, (d + 1) * width)
            p = k_ref[span, lanes].astype(f32) * v_ref[span, lanes].astype(f32)
            conv = cs_recv[d, span, :].astype(f32)
            g_ref[there, lanes] = (
                q_ref[span, lanes].astype(f32) * (conv + skip_ref[:, lanes] * p)
            ).astype(bf16)
        swap = remote(g_ref.at[there], g_ref.at[there], g_s.at[h], g_r.at[h], sibling)
        swap.start()
        swaps.append(swap)
        swap.wait_recv()
        for p in range(chunks // 2):
            if h == 0:
                own[p].wait()
            product(p, slice(h * rows, (h + 1) * rows))

    queue = [unit for p in range(chunks // 2) for unit in units[p]]

    def drain(left):
        while len(queue) > left:
            finish(queue.pop(0))

    for p in range(chunks // 2, 2 * chunks):
        if p >= 6:
            drain(0)
        if units[p] not in early:
            for kind, j in units[p]:
                weight_ready(kind, j)
        elif early.index(units[p]) >= EARLY:
            pass_on(early.index(units[p]))
        product(p, whole)
        release(p)
        drain(0)
        queue += list(units[p])
    release(2 * chunks)
    drain(0)

    side = jnp.where(z % 2 == core, it, 1 - it)
    last = []

    def total(j, whose):
        parts = []
        for h in range(2):
            span = pl.ds(pl.multiple_of(h * rows + whose * half, half), half)
            s = p_own[j, span, :] + p_recv[0, j, span, :].astype(f32)
            parts.append((s + p_recv[1, j, span, :].astype(f32)).astype(bf16))
        return jnp.concatenate(parts, axis=0)

    for j in range(chunks):
        for slot in range(2):
            remote(p_send.at[0, j], p_recv.at[slot, j], p_s.at[0, j], p_r.at[slot, j], sibling).wait_recv()
        o_send[j] = total(j, 1 - core)
        copy = remote(o_send.at[j], o_recv.at[j], o_s.at[j], o_r.at[j], sibling)
        copy.start()
        last.append(copy)
        out_ref[:, pl.ds(pl.multiple_of(side * cols + j * LANES, LANES), LANES)] = total(j, core)
    for j in range(chunks):
        last[j].wait()
        out_ref[:, pl.ds(pl.multiple_of((1 - side) * cols + j * LANES, LANES), LANES)] = o_recv[j]

    for copy in entry + back[0] + back[1] + swaps:
        copy.wait_send()
    for j in range(chunks):
        weight_x(j).wait_send()
        weight_y(j).wait_send()
        weight_on(j).wait_send()
        for kind in range(4):
            c = goal[kind]

            @pl.when(c != z)
            def _():
                remote(p_send.at[c, j], p_send.at[c, j], p_s.at[c, j], p_r.at[0, j], sibling).wait_send()


def fused(query_gate, key_proj, value_proj, filters, skip_gain, w_out):
    rows, channels = key_proj.shape
    cols = w_out.shape[1]
    blocks = lax.axis_size(SEQ)
    depth = lax.axis_size("ch")
    width = channels // blocks
    _, base, twid = tables(blocks, rows)
    cos_hi, cos_lo, sin_hi, sin_lo = base
    base = np.stack(
        [np.concatenate([cos_hi, cos_lo, cos_hi], axis=1), np.concatenate([sin_hi, sin_lo, sin_hi], axis=1)]
    )
    base = base.reshape(2, 2, rows // 2, 3 * rows).swapaxes(0, 1).reshape(2 * rows, 3 * rows)
    twid = np.pad(twid.transpose(1, 2, 0).reshape(rows, -1), ((0, 0), (0, LANES - 2 * (blocks + 1))))
    chunks = cols // LANES
    bf16, f32 = jnp.bfloat16, jnp.float32
    dma = pltpu.SemaphoreType.DMA
    anywhere, vmem = pl.BlockSpec(memory_space=pl.ANY), pl.BlockSpec(memory_space=pltpu.VMEM)
    return pl.pallas_call(
        layer_kernel,
        out_shape=jax.ShapeDtypeStruct((rows, channels), bf16),
        in_specs=[anywhere] * 4 + [vmem] + [anywhere] * 3,
        out_specs=vmem,
        scratch_shapes=[
            pltpu.VMEM((rows, channels), bf16),
            pltpu.VMEM((rows, channels), bf16),
            pltpu.VMEM((rows, channels), bf16),
            pltpu.VMEM((rows, channels), f32),
            pltpu.VMEM(base.shape, bf16),
            pltpu.VMEM(twid.shape, f32),
            pltpu.VMEM((2, blocks + 1, rows, LANES), f32),
            pltpu.VMEM((2, blocks - 1, rows, width), bf16),
            pltpu.VMEM((2, blocks, rows, width), bf16),
            pltpu.VMEM((blocks + 1, 3 * rows, 2 * width), bf16),
            pltpu.VMEM((blocks + 1, 3 * rows, 2 * width), bf16),
            pltpu.VMEM((2, blocks + 1, rows, width), f32),
            pltpu.VMEM((2, blocks + 1, rows, width), f32),
            pltpu.VMEM((blocks, rows, width), bf16),
            pltpu.VMEM((blocks, rows, width), bf16),
            pltpu.VMEM((2 * rows, channels), bf16),
            pltpu.VMEM((2 * chunks, channels, 2 * LANES), bf16),
            pltpu.VMEM((depth, chunks, 2 * rows, LANES), bf16),
            pltpu.VMEM((2, chunks, 2 * rows, LANES), bf16),
            pltpu.VMEM((chunks, 2 * rows, LANES), f32),
            pltpu.VMEM((2, chunks, 2 * rows, LANES), f32),
            pltpu.VMEM((2, chunks, 2 * rows, LANES), bf16),
            pltpu.VMEM((chunks, rows, LANES), bf16),
            pltpu.VMEM((chunks, rows, LANES), bf16),
            dma((6,)), dma((chunks,)),
            dma((2, blocks - 1)), dma((2, blocks - 1)),
            dma((2, blocks - 1)), dma((2, blocks - 1)),
            dma((2,)), dma((2,)),
            dma((3, chunks)), dma((4, chunks)),
            dma((depth, chunks)), dma((2, chunks)), dma((2, chunks)),
            dma((chunks,)), dma((chunks,)),
        ],
        compiler_params=pltpu.CompilerParams(
            collective_id=0, has_side_effects=True, vmem_limit_bytes=56 * 1024 * 1024
        ),
    )(query_gate, key_proj, value_proj, filters, skip_gain[None, :], w_out, jnp.asarray(base), jnp.asarray(twid))


def shards(query_gate, key_proj, value_proj, filters, skip_gain, w_out):
    rows, channels = key_proj.shape
    seq = lax.axis_size(SEQ)
    width = channels // seq
    if (width, w_out.shape[1] % 256, seq, lax.axis_size("seqb"), lax.axis_size("ch")) == (128, 0, 8, 4, 4):
        return fused(query_gate, key_proj, value_proj, filters, skip_gain, w_out)
    product = key_proj.astype(jnp.float32) * value_proj.astype(jnp.float32)
    pieces = lambda a: a.astype(jnp.bfloat16).reshape(rows, seq, width).transpose(1, 0, 2)
    stacked = jnp.concatenate([pieces(product), pieces(filters)], axis=2)
    columns = lax.all_to_all(stacked, SEQ, split_axis=0, concat_axis=0, tiled=True)
    spatial = lax.all_to_all(convolve(columns), SEQ, split_axis=0, concat_axis=0, tiled=True)
    convolved = spatial.transpose(1, 0, 2).reshape(rows, channels).astype(jnp.float32)
    gated_rows = (
        query_gate.astype(jnp.float32) * (convolved + skip_gain[None, :] * product)
    ).astype(jnp.bfloat16)
    weights = lax.all_gather(w_out, SEQ, axis=1, tiled=True)
    partial_sums = jnp.dot(gated_rows, weights, preferred_element_type=jnp.float32)
    return lax.psum_scatter(partial_sums, "ch", scatter_dimension=1, tiled=True).astype(
        jnp.bfloat16
    )


def solution(mesh):
    return jax.shard_map(
        shards,
        mesh=mesh,
        in_specs=(
            P(SEQ, "ch"),
            P(SEQ, "ch"),
            P(SEQ, "ch"),
            P(SEQ, "ch"),
            P("ch"),
            P("ch", SEQ),
        ),
        out_specs=P(SEQ, "ch"),
        check_vma=False,
    )
```

```python
import numpy as np

import jax
import jax.numpy as jnp
from jax import lax
from jax.experimental import pallas as pl
from jax.experimental.pallas import tpu as pltpu
from jax.sharding import PartitionSpec as P

SEQ = ("seqb", "seqt")


def split(x):
    hi = x.astype(jnp.bfloat16)
    return hi, (x - hi.astype(jnp.float32)).astype(jnp.bfloat16)


def dot32(m_hi, m_lo, a):
    a_hi, a_lo = split(a)
    dot = lambda p, q: jnp.dot(p, q, preferred_element_type=jnp.float32)
    return dot(m_hi, a_hi) + dot(m_lo, a_hi) + dot(m_hi, a_lo)


def conv_kernel(coef_ref, x_ref, base_ref, twid_ref, out_ref, acc_ref):
    blocks, rows, both = x_ref.shape
    width = both // 2
    k = pl.program_id(0)

    @pl.when(k == 0)
    def _():
        acc_ref[...] = jnp.zeros_like(acc_ref)

    re = jnp.zeros((rows, both), jnp.float32)
    im = jnp.zeros((rows, both), jnp.float32)
    for n in range(blocks):
        x = x_ref[n].astype(jnp.float32)
        re += coef_ref[0, k, n] * x
        im -= coef_ref[1, k, n] * x
    tc = twid_ref[0, :, 0:1]
    ts = twid_ref[0, :, 1:2]
    a = jnp.concatenate([re * tc + im * ts, im * tc - re * ts], axis=1)
    p = dot32(base_ref[0], base_ref[1], a)
    q = dot32(base_ref[2], base_ref[3], a)
    br = p[:, :both] + q[:, both:]
    bi = p[:, both:] - q[:, :both]
    sr, fr = br[:, :width], br[:, width:]
    si, fi = bi[:, :width], bi[:, width:]
    y = jnp.concatenate([sr * fr - si * fi, sr * fi + si * fr], axis=1)
    p = dot32(base_ref[0], base_ref[1], y)
    q = dot32(base_ref[2], base_ref[3], y)
    zr = p[:, :width] - q[:, width:]
    zi = p[:, width:] + q[:, :width]
    vr = zr * tc - zi * ts
    vi = zi * tc + zr * ts
    for n in range(blocks):
        acc_ref[n] += coef_ref[2, k, n] * vr - coef_ref[3, k, n] * vi

    @pl.when(k == blocks)
    def _():
        out_ref[...] = acc_ref[...].astype(out_ref.dtype)


def tables(blocks, rows):
    period = 2 * blocks * rows
    k = np.arange(blocks + 1)
    n = np.arange(blocks)
    ang = 2 * np.pi * ((k[:, None] * n[None, :]) % (2 * blocks)) / (2 * blocks)
    gain = np.where((k == 0) | (k == blocks), 1.0, 2.0)[:, None] / period
    coef = np.stack([np.cos(ang), np.sin(ang), gain * np.cos(ang), gain * np.sin(ang)])
    r = np.arange(rows)
    ang = 2 * np.pi * ((r[:, None] * r[None, :]) % rows) / rows
    parts = []
    for m in (np.cos(ang), np.sin(ang)):
        hi = m.astype(jnp.bfloat16)
        parts += [hi, (m - hi.astype(np.float64)).astype(jnp.bfloat16)]
    ang = 2 * np.pi * ((k[:, None] * r[None, :]) % period) / period
    twid = np.stack([np.cos(ang), np.sin(ang)], axis=-1)
    return coef.astype(np.float32), np.stack(parts), twid.astype(np.float32)


def convolve(columns):
    blocks, rows, both = columns.shape
    coef, base, twid = tables(blocks, rows)
    return pl.pallas_call(
        conv_kernel,
        grid=(blocks + 1,),
        out_shape=jax.ShapeDtypeStruct((blocks, rows, both // 2), jnp.bfloat16),
        in_specs=[
            pl.BlockSpec(memory_space=pltpu.SMEM),
            pl.BlockSpec((blocks, rows, both), lambda k: (0, 0, 0)),
            pl.BlockSpec((4, rows, rows), lambda k: (0, 0, 0)),
            pl.BlockSpec((1, rows, 2), lambda k: (k, 0, 0)),
        ],
        out_specs=pl.BlockSpec((blocks, rows, both // 2), lambda k: (0, 0, 0)),
        scratch_shapes=[pltpu.VMEM((blocks, rows, both // 2), jnp.float32)],
        compiler_params=pltpu.CompilerParams(vmem_limit_bytes=48 * 1024 * 1024),
        cost_estimate=pl.CostEstimate(
            flops=36 * (blocks + 1) * rows * rows * both, bytes_accessed=4 * 1024 * 1024, transcendentals=0
        ),
    )(jnp.asarray(coef), columns, jnp.asarray(base), jnp.asarray(twid))


MESH = pl.DeviceIdType.MESH
LANES = 128
HALF = float(np.sqrt(0.5))
COS = [float(np.cos(np.pi * n / 8)) for n in range(4)]
SIN = [float(np.sin(np.pi * n / 8)) for n in range(4)]


def forward16(x):
    a = [x[n] + x[n + 4] for n in range(4)]
    b = [x[n] - x[n + 4] for n in range(4)]
    s, t = a[0] + a[2], a[1] + a[3]
    u, w = HALF * (b[1] - b[3]), HALF * (b[1] + b[3])
    even = {
        0: (s + t, None),
        8: (s - t, None),
        4: (a[0] - a[2], a[3] - a[1]),
        2: (b[0] + u, -b[2] - w),
        6: (b[0] - u, b[2] - w),
    }
    ur, ui = [x[0]], [-x[4]]
    for n in range(1, 4):
        ur.append(COS[n] * x[n] - SIN[n] * x[n + 4])
        ui.append(-COS[n] * x[n + 4] - SIN[n] * x[n])
    t0r, t0i, t1r, t1i = ur[0] + ur[2], ui[0] + ui[2], ur[0] - ur[2], ui[0] - ui[2]
    t2r, t2i, t3r, t3i = ur[1] + ur[3], ui[1] + ui[3], ur[1] - ur[3], ui[1] - ui[3]
    odd = {
        1: (t0r + t2r, t0i + t2i),
        7: (t0r - t2r, t2i - t0i),
        5: (t1r + t3i, t1i - t3r),
        3: (t1r - t3i, -t1i - t3r),
    }
    return {**even, **odd}


def backward16(re, im):
    s, t = re[0] + re[8], re[0] - re[8]
    p = [s + re[4], t - im[4], s - re[4], t + im[4]]
    u, w = HALF * (re[2] - re[6]), HALF * (im[2] + im[6])
    q = [re[2] + re[6], u - w, im[6] - im[2], -u - w]
    w1r, w1i, w5r, w5i = re[1], im[1], re[5], im[5]
    w9r, w9i, w13r, w13i = re[7], -im[7], re[3], -im[3]
    ar, ai, br, bi = w1r + w9r, w1i + w9i, w1r - w9r, w1i - w9i
    cr, ci, dr, di = w5r + w13r, w5i + w13i, w5r - w13r, w5i - w13i
    gr = [ar + cr, br - di, ar - cr, br + di]
    gi = [ai + ci, bi + dr, ai - ci, bi - dr]
    low, high = [], []
    for n in range(4):
        if n == 0:
            o, r = gr[0], -gi[0]
        else:
            o = COS[n] * gr[n] - SIN[n] * gi[n]
            r = -COS[n] * gi[n] - SIN[n] * gr[n]
        low.append(p[n] + q[n] + o)
        high.append(p[n] - q[n] + r)
    return low + high


def layer_kernel(q_hbm, k_hbm, v_hbm, f_hbm, skip_ref, w_hbm, base_hbm, twid_hbm, out_hbm,
                 out_ref, q_ref, k_ref, v_ref, f_ref, base_ref, angle_ref, twid_ref,
                 xs_send, xs_recv, a_ref, y_ref, f_spec, v_spec, cs_send, cs_recv, g_ref, w_all,
                 p_send, p_recv, p_own, p_far, r_recv, o_send, o_recv,
                 load_s, own_s, in_s, in_r, back_s, back_r, g_s, g_r, w_s, w_r,
                 p_s, p_r, r_r, o_s, o_r, half_r, out_s):
    blocks = lax.axis_size("seqb") * lax.axis_size("seqt")
    depth = lax.axis_size("ch")
    ib, it, z = lax.axis_index("seqb"), lax.axis_index("seqt"), lax.axis_index("ch")
    me = ib * 2 + it
    core, chip = ib % 2, ib // 2
    rows, channels = k_ref.shape
    width = channels // blocks
    cols = w_hbm.shape[1]
    chunks = cols // LANES
    half = rows // 2
    f32, bf16 = jnp.float32, jnp.bfloat16
    flips = [ib, ib + 1 - 2 * core, (ib + 2) % 4, 3 - ib]
    peers = [(a, t) for a, t in ((2, 1), (3, 1), (2, 0), (0, 1), (3, 0), (1, 1), (1, 0))]
    place = [{"seqb": flips[a], "seqt": it if t == 0 else 1 - it} for a, t in peers]
    index = [flips[a] * 2 + (it if t == 0 else 1 - it) for a, t in peers]
    sibling = {"seqb": flips[1]}
    over_x = {"seqb": flips[2]}
    over_y = {"seqb": flips[1], "seqt": 1 - it}

    def remote(src, dst, send, recv, where):
        return pltpu.make_async_remote_copy(
            src_ref=src, dst_ref=dst, send_sem=send, recv_sem=recv, device_id=where, device_id_type=MESH
        )

    loads = [
        pltpu.make_async_copy(src, dst, load_s.at[i])
        for i, (src, dst) in enumerate(
            ((f_hbm, f_ref), (k_hbm, k_ref), (v_hbm, v_ref), (twid_hbm, angle_ref), (base_hbm, base_ref), (q_hbm, q_ref))
        )
    ]
    x_order = list(range(chunks // 2, chunks)) + list(range(chunks // 2))
    y_order = list(range(chunks))
    units = [((0, 2 * i), (0, 2 * i + 1)) for i in range(chunks // 2)]
    straight = [((1, x_order[i]), (2, y_order[i])) for i in range(chunks)]
    diagonal = [((3, i), (3, chunks // 2 + i)) for i in range(chunks // 2)]
    early, late = straight[:chunks // 2], straight[chunks // 2:]
    units += early + [pair for both in zip(diagonal, late) for pair in both]

    def store(kind, j):
        for p, pair in enumerate(units):
            if (kind, j) in pair:
                return w_all.at[p, :, pl.ds(pair.index((kind, j)) * LANES, LANES)]

    own = [
        pltpu.make_async_copy(w_hbm.at[:, pl.ds(2 * i * LANES, 2 * LANES)], w_all.at[i], own_s.at[i])
        for i in range(chunks // 2)
    ]
    for copy in loads:
        copy.start()

    barrier = pltpu.get_barrier_semaphore()
    for where in place:
        pl.semaphore_signal(barrier, inc=1, device_id=where, device_id_type=MESH)
    for j in range(1, depth):
        pl.semaphore_signal(barrier, inc=1, device_id={"ch": (z + j) % depth}, device_id_type=MESH)

    def lanes_of(d):
        return pl.ds(pl.multiple_of(d * width, width), width)

    def filter_piece(d):
        return f_ref[:, lanes_of(d)].astype(bf16)

    def product_piece(d):
        return (k_ref[:, lanes_of(d)].astype(f32) * v_ref[:, lanes_of(d)].astype(f32)).astype(bf16)

    entry = []
    for s, piece in enumerate((filter_piece, product_piece)):
        for copy in loads[:1] if s == 0 else loads[1:3]:
            copy.wait()
        for i in range(len(peers)):
            xs_send[s, i] = piece(index[i])
        if s == 0:
            pl.semaphore_wait(barrier, blocks + depth - 2)
        for i in range(len(peers)):
            copy = remote(xs_send.at[s, i], xs_recv.at[s, me], in_s.at[s, i], in_r.at[s, i], place[i])
            copy.start()
            entry.append(copy)
        xs_recv[s, me] = piece(me)
    for copy in own:
        copy.start()

    def weight_x(j):
        return remote(w_hbm.at[:, pl.ds(j * LANES, LANES)], store(1, j), w_s.at[0, j], w_r.at[1, j], over_x)

    def weight_y(j):
        return remote(w_hbm.at[:, pl.ds(j * LANES, LANES)], store(2, j), w_s.at[1, j], w_r.at[2, j], over_y)

    def weight_on(j):
        if j < chunks // 2:
            return remote(store(2, j), store(3, j), w_s.at[2, j], w_r.at[3, j], over_x)
        return remote(store(1, j), store(3, j), w_s.at[2, j], w_r.at[3, j], over_y)

    def weight_ready(kind, j):
        remote(store(kind, j), store(kind, j), w_s.at[0, j], w_r.at[kind, j], over_x).wait_recv()

    EARLY = 1
    for j in range(EARLY):
        weight_x(x_order[j]).start()
        weight_y(y_order[j]).start()

    loads[3].wait()
    for c in range(2):
        for k in range(blocks + 1):
            column = c * (blocks + 1) + k
            twid_ref[c, k] = jnp.broadcast_to(angle_ref[:, column:column + 1], (rows, LANES))
    loads[4].wait()

    tile = 16

    def put(dst, k, start, lane, value):
        hi, lo = split(value)
        span = slice(lane * LANES, (lane + 1) * LANES)
        dst[k, pl.ds(start, tile), span] = hi
        dst[k, pl.ds(rows + start, tile), span] = hi
        dst[k, pl.ds(2 * rows + start, tile), span] = lo

    def spread(s):
        def body(i, carry):
            start = pl.multiple_of(i * tile, tile)
            span = pl.ds(start, tile)
            out = forward16([xs_recv[s, n, span, :].astype(f32) for n in range(blocks)])
            for k in range(blocks + 1):
                re, im = out[k]
                if k == 0:
                    im = jnp.zeros_like(re)
                else:
                    tc, ts = twid_ref[0, k, span, :], twid_ref[1, k, span, :]
                    if im is None:
                        re, im = re * tc, -re * ts
                    else:
                        re, im = re * tc + im * ts, im * tc - re * ts
                put(a_ref, k, start, 0, re)
                put(a_ref, k, start, 1, im)
            return carry

        lax.fori_loop(0, rows // tile, body, 0)

    def transform(value, h):
        d = jnp.dot(base_ref[h * rows:(h + 1) * rows], value, preferred_element_type=f32)
        return d[:half, :LANES], d[:half, LANES:], d[half:, :LANES], d[half:, LANES:]

    for copy in entry[: len(peers)]:
        copy.wait_recv()
    spread(0)
    scale = 1.0 / (2 * blocks * rows)

    def filter_step(k):
        for h in range(2):
            span = slice(h * half, (h + 1) * half)
            cr, ci, sr, si = transform(a_ref[k], h)
            gain = scale if k in (0, blocks) else 2 * scale
            f_spec[0, k, span] = (cr + si) * gain
            f_spec[1, k, span] = (ci - sr) * gain

    for k in range(blocks + 1):
        filter_step(k)

    for copy in entry[len(peers):]:
        copy.wait_recv()
    spread(1)

    def signal_step(k):
        for h in range(2):
            span = slice(h * half, (h + 1) * half)
            cr, ci, sr, si = transform(a_ref[k], h)
            xr, xi = cr + si, ci - sr
            fr, fi = f_spec[0, k, span], f_spec[1, k, span]
            for e, y in enumerate((xr * fr - xi * fi, xr * fi + xi * fr)):
                lanes = slice(e * LANES, (e + 1) * LANES)
                hi, lo = split(y)
                y_ref[k, h * half:(h + 1) * half, lanes] = hi
                y_ref[k, rows + h * half:rows + (h + 1) * half, lanes] = hi
                y_ref[k, 2 * rows + h * half:2 * rows + (h + 1) * half, lanes] = lo

    def inverse_step(k, h):
        span = slice(h * half, (h + 1) * half)
        cr, ci, sr, si = transform(y_ref[k], h)
        zr, zi = cr - si, ci + sr
        tc, ts = twid_ref[0, k, span], twid_ref[1, k, span]
        v_spec[0, k, span] = zr * tc - zi * ts
        v_spec[1, k, span] = zi * tc + zr * ts

    for k in range(blocks + 1):
        signal_step(k)

    def gather_points(h):
        def body(i, carry):
            span = pl.ds(pl.multiple_of(h * half + i * tile, tile), tile)
            re = [v_spec[0, k, span, :] for k in range(blocks + 1)]
            im = [v_spec[1, k, span, :] for k in range(blocks + 1)]
            for n, value in enumerate(backward16(re, im)):
                cs_send[n, span, :] = value.astype(bf16)
            return carry

        lax.fori_loop(0, half // tile, body, 0)

    back = [[], []]
    for h in range(2):
        for k in range(blocks + 1):
            inverse_step(k, h)
        gather_points(h)
        span = pl.ds(h * half, half)
        for i in range(len(peers)):
            copy = remote(
                cs_send.at[index[i], span], cs_recv.at[me, span], back_s.at[h, i], back_r.at[h, i], place[i]
            )
            copy.start()
            back[h].append(copy)
        cs_recv[me, span] = cs_send[me, span]
    pending = []
    for i in range(chunks // 2):
        pending += [(weight_on(y_order[i]), weight_on(x_order[i]))]
        pending += [(weight_x(x_order[chunks // 2 + i]), weight_y(y_order[chunks // 2 + i]))]
    for i in range(EARLY, chunks // 2):
        weight_x(x_order[i]).start()
        weight_y(y_order[i]).start()

    def pass_on(i):
        for kind, j in early[i]:
            weight_ready(kind, j)
        for pair in pending[2 * i:2 * i + 2]:
            for copy in pair:
                copy.start()

    for i in range(EARLY):
        pass_on(i)

    goal = [chip * 2 + core, (1 - chip) * 2 + core, chip * 2 + 1 - core, (1 - chip) * 2 + 1 - core]
    beside = z + 1 - 2 * (z % 2)
    outer = (z == 0) | (z == 3)
    inner = jnp.logical_not(outer)
    whole = slice(0, 2 * rows)

    def direct(c, j, span=whole):
        slot = jnp.where(c == beside, 0, 1)
        return remote(
            p_send.at[c, j, span], p_recv.at[slot, j, span], p_s.at[c, j], p_r.at[slot, j], {"ch": c}
        )

    def relay(c, j, span=whole, landed=None):
        landed = r_r.at[c % 2, j] if landed is None else landed
        return remote(
            p_send.at[c, j, span], r_recv.at[c % 2, j, span], p_s.at[c, j], landed, {"ch": beside}
        )

    halves = [slice(h * rows, (h + 1) * rows) for h in range(2)]

    def finish(unit):
        kind, j = unit
        c = goal[kind]
        last = unit in units[-1]

        @pl.when(inner & (c != z) & (c != beside))
        def _():
            for h, span in enumerate(halves if last else [whole]):
                relay(c, j, span, half_r.at[kind - 1, h] if last else None).wait_recv()
                p_send[c, j, span] = (p_far[c % 2, j, span] + r_recv[c % 2, j, span].astype(f32)).astype(bf16)
                direct(c, j, span).start()

    def product(p, span, h=0):
        last = p == len(units) - 1
        both = jnp.dot(g_ref[span], w_all[p], preferred_element_type=f32)
        for e, (kind, j) in enumerate(units[p]):
            part = both[:, e * LANES:(e + 1) * LANES]
            c = goal[kind]

            @pl.when(c == z)
            def _():
                p_own[j, span] = part

            @pl.when(inner & (c != z) & (c != beside))
            def _():
                p_far[c % 2, j, span] = part

            @pl.when((outer & (c != z)) | (c == beside))
            def _():
                p_send[c, j, span] = part.astype(bf16)

            @pl.when((c == beside) & inner if p in held else c == beside)
            def _():
                direct(c, j, span).start()

            @pl.when(outer & (c != z) & (c != beside))
            def _():
                relay(c, j, span, half_r.at[kind - 1, h] if last else None).start()

    held = {1: 3, 2: 4, 3: 5, 4: 6, 5: 7, 6: 8, 7: 8}

    def release(step):
        for p in held:
            if held[p] == step:
                for kind, j in units[p]:
                    @pl.when(outer & (goal[kind] == beside))
                    def _():
                        direct(goal[kind], j).start()

    loads[5].wait()
    swaps = []
    for h in range(2):
        for copy in back[h]:
            copy.wait_recv()
        span = slice(h * half, (h + 1) * half)
        there = pl.ds(pl.multiple_of(h * rows + core * half, half), half)
        for d in range(blocks):
            lanes = slice(d * width, (d + 1) * width)
            p = k_ref[span, lanes].astype(f32) * v_ref[span, lanes].astype(f32)
            conv = cs_recv[d, span, :].astype(f32)
            g_ref[there, lanes] = (
                q_ref[span, lanes].astype(f32) * (conv + skip_ref[:, lanes] * p)
            ).astype(bf16)
        swap = remote(g_ref.at[there], g_ref.at[there], g_s.at[h], g_r.at[h], sibling)
        swap.start()
        swaps.append(swap)
        for p in range(chunks // 2):
            if h == 0:
                own[p].wait()
            product(p, there)
        swap.wait_recv()
        for p in range(chunks // 2):
            product(p, pl.ds(pl.multiple_of((2 * h + 1 - core) * half, half), half))

    queue = [unit for p in range(chunks // 2) for unit in units[p]]

    def drain(left):
        while len(queue) > left:
            finish(queue.pop(0))

    for p in range(chunks // 2, 2 * chunks):
        if p >= 6:
            drain(0)
        if units[p] not in early:
            for kind, j in units[p]:
                weight_ready(kind, j)
        elif early.index(units[p]) >= EARLY:
            pass_on(early.index(units[p]))
        if p < 2 * chunks - 1:
            product(p, whole)
        else:
            for h in range(2):
                product(p, halves[h], h)
        release(p)
        drain(0)
        queue += list(units[p])
    release(2 * chunks)
    drain(0)

    side = jnp.where(z % 2 == core, it, 1 - it)

    def write(where, n):
        lanes = pl.ds(pl.multiple_of(where * cols, cols), cols)
        return pltpu.make_async_copy(out_ref.at[:, lanes], out_hbm.at[:, lanes], out_s.at[n])

    def exchange(j):
        return remote(o_send.at[j], o_recv.at[j], o_s.at[j], o_r.at[j], sibling)

    def total(j, whose):
        parts = []
        for h in range(2):
            span = pl.ds(pl.multiple_of(h * rows + whose * half, half), half)
            s = p_own[j, span, :] + p_recv[0, j, span, :].astype(f32)
            parts.append((s + p_recv[1, j, span, :].astype(f32)).astype(bf16))
        return jnp.concatenate(parts, axis=0)

    x_kind = goal[1] == z
    for i in range(chunks):
        j = jnp.where(x_kind, x_order[i], y_order[i])
        for slot in range(2):
            remote(p_send.at[0, j], p_recv.at[slot, j], p_s.at[0, j], p_r.at[slot, j], sibling).wait_recv()
        o_send[j] = total(j, 1 - core)
        exchange(j).start()
        out_ref[:, pl.ds(pl.multiple_of(side * cols + j * LANES, LANES), LANES)] = total(j, core)
    write(side, 0).start()
    for j in range(chunks):
        exchange(j).wait()
        out_ref[:, pl.ds(pl.multiple_of((1 - side) * cols + j * LANES, LANES), LANES)] = o_recv[j]
    write(1 - side, 1).start()
    for n in range(2):
        write(n, n).wait()

    for copy in entry + back[0] + back[1] + swaps:
        copy.wait_send()
    for j in range(chunks):
        weight_x(j).wait_send()
        weight_y(j).wait_send()
        weight_on(j).wait_send()
        for kind in range(4):
            c = goal[kind]

            @pl.when(c != z)
            def _():
                remote(p_send.at[c, j], p_send.at[c, j], p_s.at[c, j], p_r.at[0, j], sibling).wait_send()


def fused(query_gate, key_proj, value_proj, filters, skip_gain, w_out):
    rows, channels = key_proj.shape
    cols = w_out.shape[1]
    blocks = lax.axis_size(SEQ)
    depth = lax.axis_size("ch")
    width = channels // blocks
    _, base, twid = tables(blocks, rows)
    cos_hi, cos_lo, sin_hi, sin_lo = base
    base = np.stack(
        [np.concatenate([cos_hi, cos_lo, cos_hi], axis=1), np.concatenate([sin_hi, sin_lo, sin_hi], axis=1)]
    )
    base = base.reshape(2, 2, rows // 2, 3 * rows).swapaxes(0, 1).reshape(2 * rows, 3 * rows)
    twid = np.pad(twid.transpose(1, 2, 0).reshape(rows, -1), ((0, 0), (0, LANES - 2 * (blocks + 1))))
    chunks = cols // LANES
    bf16, f32 = jnp.bfloat16, jnp.float32
    dma = pltpu.SemaphoreType.DMA
    anywhere, vmem = pl.BlockSpec(memory_space=pl.ANY), pl.BlockSpec(memory_space=pltpu.VMEM)
    return pl.pallas_call(
        layer_kernel,
        out_shape=jax.ShapeDtypeStruct((rows, channels), bf16),
        in_specs=[anywhere] * 4 + [vmem] + [anywhere] * 3,
        out_specs=anywhere,
        scratch_shapes=[
            pltpu.VMEM((rows, channels), bf16),
            pltpu.VMEM((rows, channels), bf16),
            pltpu.VMEM((rows, channels), bf16),
            pltpu.VMEM((rows, channels), bf16),
            pltpu.VMEM((rows, channels), f32),
            pltpu.VMEM(base.shape, bf16),
            pltpu.VMEM(twid.shape, f32),
            pltpu.VMEM((2, blocks + 1, rows, LANES), f32),
            pltpu.VMEM((2, blocks - 1, rows, width), bf16),
            pltpu.VMEM((2, blocks, rows, width), bf16),
            pltpu.VMEM((blocks + 1, 3 * rows, 2 * width), bf16),
            pltpu.VMEM((blocks + 1, 3 * rows, 2 * width), bf16),
            pltpu.VMEM((2, blocks + 1, rows, width), f32),
            pltpu.VMEM((2, blocks + 1, rows, width), f32),
            pltpu.VMEM((blocks, rows, width), bf16),
            pltpu.VMEM((blocks, rows, width), bf16),
            pltpu.VMEM((2 * rows, channels), bf16),
            pltpu.VMEM((2 * chunks, channels, 2 * LANES), bf16),
            pltpu.VMEM((depth, chunks, 2 * rows, LANES), bf16),
            pltpu.VMEM((2, chunks, 2 * rows, LANES), bf16),
            pltpu.VMEM((chunks, 2 * rows, LANES), f32),
            pltpu.VMEM((2, chunks, 2 * rows, LANES), f32),
            pltpu.VMEM((2, chunks, 2 * rows, LANES), bf16),
            pltpu.VMEM((chunks, rows, LANES), bf16),
            pltpu.VMEM((chunks, rows, LANES), bf16),
            dma((6,)), dma((chunks,)),
            dma((2, blocks - 1)), dma((2, blocks - 1)),
            dma((2, blocks - 1)), dma((2, blocks - 1)),
            dma((2,)), dma((2,)),
            dma((3, chunks)), dma((4, chunks)),
            dma((depth, chunks)), dma((2, chunks)), dma((2, chunks)),
            dma((chunks,)), dma((chunks,)), dma((2, 2)), dma((2,)),
        ],
        compiler_params=pltpu.CompilerParams(
            collective_id=0, has_side_effects=True, vmem_limit_bytes=56 * 1024 * 1024
        ),
    )(query_gate, key_proj, value_proj, filters, skip_gain[None, :], w_out, jnp.asarray(base), jnp.asarray(twid))


def shards(query_gate, key_proj, value_proj, filters, skip_gain, w_out):
    rows, channels = key_proj.shape
    seq = lax.axis_size(SEQ)
    width = channels // seq
    if (width, w_out.shape[1] % 256, seq, lax.axis_size("seqb"), lax.axis_size("ch")) == (128, 0, 8, 4, 4):
        return fused(query_gate, key_proj, value_proj, filters, skip_gain, w_out)
    product = key_proj.astype(jnp.float32) * value_proj.astype(jnp.float32)
    pieces = lambda a: a.astype(jnp.bfloat16).reshape(rows, seq, width).transpose(1, 0, 2)
    stacked = jnp.concatenate([pieces(product), pieces(filters)], axis=2)
    columns = lax.all_to_all(stacked, SEQ, split_axis=0, concat_axis=0, tiled=True)
    spatial = lax.all_to_all(convolve(columns), SEQ, split_axis=0, concat_axis=0, tiled=True)
    convolved = spatial.transpose(1, 0, 2).reshape(rows, channels).astype(jnp.float32)
    gated_rows = (
        query_gate.astype(jnp.float32) * (convolved + skip_gain[None, :] * product)
    ).astype(jnp.bfloat16)
    weights = lax.all_gather(w_out, SEQ, axis=1, tiled=True)
    partial_sums = jnp.dot(gated_rows, weights, preferred_element_type=jnp.float32)
    return lax.psum_scatter(partial_sums, "ch", scatter_dimension=1, tiled=True).astype(
        jnp.bfloat16
    )


def solution(mesh):
    return jax.shard_map(
        shards,
        mesh=mesh,
        in_specs=(
            P(SEQ, "ch"),
            P(SEQ, "ch"),
            P(SEQ, "ch"),
            P(SEQ, "ch"),
            P("ch"),
            P("ch", SEQ),
        ),
        out_specs=P(SEQ, "ch"),
        check_vma=False,
    )
```
